32 devices in a mesh: exp: 8 (over z, x), tp: 4 (over y, core).
Axes of the slice: x: 2, y: 2, z: 4, core: 2. Of those that a mesh axis runs over, the one named last changes fastest.
Arguments:
- tokens: bfloat16 [4096, 2048], P(('exp', 'tp')), may hold values from -6 to 6
- cotangent: bfloat16 [4096, 2048], P(('exp', 'tp')), may hold values from -6 to 6
- attention_gain: float32 [2048], replicated, may hold values from 0.5 to 1.5
- query_weight: bfloat16 [2048, 2048], P(None, 'tp'), may hold values from -0.125 to 0.125
- key_weight: bfloat16 [2048, 2048], P(None, 'tp'), may hold values from -0.125 to 0.125
- value_weight: bfloat16 [2048, 2048], P(None, 'tp'), may hold values from -0.125 to 0.125
- output_weight: bfloat16 [2048, 2048], P('tp'), may hold values from -1 to 1
- query_norm: float32 [2048], P('tp'), may hold values from 0.5 to 1.5
- key_norm: float32 [2048], P('tp'), may hold values from 0.5 to 1.5
- mixture_gain: float32 [2048], replicated, may hold values from 0.5 to 1.5
- router_weight: bfloat16 [2048, 16], replicated, may hold values from -0.0625 to 0.0625
- gate_weight: bfloat16 [16, 2048, 1024], P('exp', None, 'tp'), may hold values from -0.125 to 0.125
- up_weight: bfloat16 [16, 2048, 1024], P('exp', None, 'tp'), may hold values from -0.125 to 0.125
- down_weight: bfloat16 [16, 1024, 2048], P('exp', 'tp'), may hold values from -3 to 3
- routes: int32 [4096, 8], P(('exp', 'tp')), may hold values from 0 to 15, all different within a row
- segments: int32 [8, 512], P('exp'), may hold values from 0 to 3, never falling along the last dimension, each value on 1 to 256 neighbouring positions
Outputs:
- output: bfloat16 [4096, 2048], P(('exp', 'tp'))
- tokens_grad: float32 [4096, 2048], P(('exp', 'tp'))
- attention_gain_grad: float32 [2048], replicated
- query_weight_grad: float32 [2048, 2048], P(None, 'tp')
- key_weight_grad: float32 [2048, 2048], P(None, 'tp')
- value_weight_grad: float32 [2048, 2048], P(None, 'tp')
- output_weight_grad: float32 [2048, 2048], P('tp')
- query_norm_grad: float32 [2048], P('tp')
- key_norm_grad: float32 [2048], P('tp')
- mixture_gain_grad: float32 [2048], replicated
- router_weight_grad: float32 [2048, 16], replicated
- gate_weight_grad: float32 [16, 2048, 1024], P('exp', None, 'tp')
- up_weight_grad: float32 [16, 2048, 1024], P('exp', None, 'tp')
- down_weight_grad: float32 [16, 1024, 2048], P('exp', 'tp')
The draws below stay inside these ranges and needn't reach their ends.
Inputs may be any that keep to these rules, and one draw needn't show every extreme that they name: `routes`: each token names 8 different experts; every expert is named by some token. `segments`: in each row the ids never fall and start at 0; each of the 4 ids covers 1 to 256 consecutive positions, one exactly 256.
All inputs are finite; a program needn't handle non-finite values.
Results may differ from the reference program's by a relative error of at most 0.025.
Values may be sent and summed in bfloat16 or wider, within the bound.
No kernel may reach another device: no remote copies, remote signals or barrier semaphores. Data moves between devices by JAX's collectives and lax.ppermute only.
A program may use at most 256 MiB of HBM per device.

```python
import math
import jax
import jax.numpy as jnp
import numpy as np
from jax import lax

MODEL_DIM = 2048
H = 16
HD = 128
FF_E = 1024
TOP = 8
TOK_DEV = 128
DOCS_PER_ROW = 4
EXPERTS = 16
CAP = 56
PACKED_LENGTH = 512
PACKED_ROWS = 8
TOTAL_TOKENS = 4096
LONGEST_DOC = 256
N_EXP = 8
N_TP = 4


def levels(own_key, shape, split, least, high):
    def one(axis_at, shards_of):
        draws = jax.random.uniform(jax.random.fold_in(jax.random.fold_in(own_key, 6), axis_at), (shards_of,), jnp.float32, least / len(split), high / len(split))
        return jnp.repeat(jnp.exp(draws), shape[axis_at] // shards_of).reshape((-1,) + (1,) * (len(shape) - axis_at - 1))

    loudness = one(*split[0])
    for cut in split[1:]:
        loudness = loudness * one(*cut)
    return loudness


def distinct(rng, rows, count, top, lift):
    order = jax.random.permutation(jax.random.fold_in(rng, 1), count)
    favour = order
    for power in range(3):
        favour = favour * favour // count
    favour = favour * lift // count
    chance = jax.random.randint(jax.random.fold_in(rng, 2), (rows, count), 0, 4096) + favour
    sure = jax.random.permutation(jax.random.fold_in(rng, 3), rows)[jnp.arange(count) % rows]
    chance = jnp.where(jnp.arange(rows)[:, None] == sure[None, :], 1 << 14, chance)
    priority = chance * count + jnp.arange(count)
    return lax.top_k(priority.astype(jnp.int32), top)[1].astype(jnp.int32)


def split_up(count, total, most, slope):
    weights = [(1 << 20) // math.isqrt(grade ** slope) + 1 for grade in range(2, count + 1)]
    spare, given = total - most - (count - 1), [1] * (count - 1)
    while spare > 0:
        candidates = [i for i in range(count - 1) if given[i] < most]
        mass, left = sum([weights[i] for i in candidates]), spare
        for i in candidates:
            more = min(most - given[i], max(1, left * weights[i] // mass), spare)
            given[i] = given[i] + more
            spare = spare - more
    return np.array([most] + given)


def ragged(own_key, count, total, bound, lean):
    if count == 2:
        one = jax.random.randint(own_key, (), max(1, total - bound), min(bound, total - 1) + 1)
        return jnp.stack([one, total - one])
    lengths = jnp.asarray(split_up(count, total, bound, lean), jnp.int32)
    pairs = (count - 1) // 2
    donor, receiver = lengths[1:1 + 2 * pairs:2], lengths[2:2 + 2 * pairs:2]
    margin = jnp.minimum(donor - 1, bound - receiver)
    moved = jax.random.randint(jax.random.fold_in(own_key, 1), (pairs,), 0, 1 << 20) % (margin + 1)
    lengths = lengths.at[1:1 + 2 * pairs:2].set(donor - moved).at[2:2 + 2 * pairs:2].set(receiver + moved)
    return lengths[jax.random.permutation(jax.random.fold_in(own_key, 2), count)]


def centred(key, dims, spread, reach, shards=(), held_as=jnp.bfloat16):
    level = levels(key, dims, shards, -0.22, 0.18) if shards else 1.0
    array = jax.random.normal(key, dims, jnp.float32) * spread * level
    return jnp.minimum(jnp.maximum(array, -reach), reach).astype(held_as)


def setup_inputs(seed: int = 0) -> dict:
    seeds = jax.random.split(jax.random.key(seed), 17)
    return {
        "tokens": centred(seeds[0], (TOTAL_TOKENS, MODEL_DIM), 1.0, 6.0, ((0, 32),)),
        "cotangent": centred(seeds[1], (TOTAL_TOKENS, MODEL_DIM), 1.0, 6.0, ((0, 32),)),
        "attention_gain": jnp.clip(1.0 + 0.1 * jax.random.normal(seeds[2], (MODEL_DIM,), jnp.float32), 0.5, 1.5),
        "query_weight": centred(seeds[3], (MODEL_DIM, MODEL_DIM), MODEL_DIM ** -0.5, 0.125, ((1, 4),)),
        "key_weight": centred(seeds[4], (MODEL_DIM, MODEL_DIM), MODEL_DIM ** -0.5, 0.125, ((1, 4),)),
        "value_weight": centred(seeds[5], (MODEL_DIM, MODEL_DIM), MODEL_DIM ** -0.5, 0.125, ((1, 4),)),
        "output_weight": centred(seeds[6], (MODEL_DIM, MODEL_DIM), (MODEL_DIM // 64) ** -0.5, 1.0, ((0, 4),)),
        "query_norm": jnp.clip(1.0 + 0.1 * jax.random.normal(seeds[7], (MODEL_DIM,), jnp.float32), 0.5, 1.5),
        "key_norm": jnp.clip(1.0 + 0.1 * jax.random.normal(seeds[8], (MODEL_DIM,), jnp.float32), 0.5, 1.5),
        "mixture_gain": jnp.clip(1.0 + 0.1 * jax.random.normal(seeds[9], (MODEL_DIM,), jnp.float32), 0.5, 1.5),
        "router_weight": centred(seeds[10], (MODEL_DIM, EXPERTS), (4 * MODEL_DIM) ** -0.5, 0.0625),
        "gate_weight": centred(seeds[11], (EXPERTS, MODEL_DIM, FF_E), MODEL_DIM ** -0.5, 0.125, ((0, 8), (2, 4))),
        "up_weight": centred(seeds[12], (EXPERTS, MODEL_DIM, FF_E), MODEL_DIM ** -0.5, 0.125, ((0, 8), (2, 4))),
        "down_weight": centred(seeds[13], (EXPERTS, FF_E, MODEL_DIM), 4 ** -0.5, 3.0, ((0, 8), (1, 4))),
        "routes": distinct(seeds[14], TOTAL_TOKENS, EXPERTS, TOP, 4096),
        "segments": jax.vmap(lambda own: jnp.searchsorted(jnp.cumsum(ragged(own, DOCS_PER_ROW, PACKED_LENGTH, LONGEST_DOC, 1)), jnp.arange(PACKED_LENGTH), side="right"))(jax.random.split(seeds[15], PACKED_ROWS)).reshape((PACKED_ROWS, PACKED_LENGTH)).astype(jnp.int32),
    }


@jax.custom_vjp
def low(v):
    return lax.optimization_barrier(v.astype(jnp.bfloat16)).astype(jnp.float32)

@jax.custom_vjp
def low_back(v):
    return v

def low_keep(v):
    return (low(v), None)

def low_pass(kept, grad):
    return (grad,)

def back_keep(v):
    return (v, None)

def back_low(kept, grad):
    return (low(grad),)
low.defvjp(low_keep, low_pass)
low_back.defvjp(back_keep, back_low)
EPS = 1e-05
HIGH = lax.Precision.HIGHEST

def matmul_high(first_arg, second_arg):
    return jnp.matmul(first_arg, second_arg, precision=HIGH)

def rms_norm(values, gain):
    return values * lax.rsqrt(lax.optimization_barrier(jnp.mean(values * values, axis=-1, keepdims=True)) + EPS) * gain

def positions_of(segment_row):
    earlier = lax.optimization_barrier(jnp.sum((segment_row[None, :] < segment_row[:, None]).astype(jnp.int32), axis=1))
    return jnp.arange(segment_row.shape[0], dtype=jnp.int32) - earlier

def rope_tables(positions):
    half_dim = HD // 2
    inverse_freq = 10000.0 ** (-2.0 * jnp.arange(half_dim).astype(jnp.float32) / HD)
    angles = positions.astype(jnp.float32)[:, None] * inverse_freq[None, :]
    return (jnp.cos(angles)[:, None, :], jnp.sin(angles)[:, None, :])

def rotate(values, cos_table, sin_table):
    half_dim = values.shape[-1] // 2
    first_half = values[..., :half_dim]
    second_half = values[..., half_dim:]
    return jnp.concatenate([first_half * cos_table - second_half * sin_table, second_half * cos_table + first_half * sin_table], axis=-1)

def attend_row(row_inputs, segment_row, w_query, w_key, w_value, w_output, norm_query, norm_key):
    row_length = row_inputs.shape[0]
    queries = low_back(matmul_high(row_inputs, w_query)).reshape(row_length, H, HD)
    key_rows = low_back(matmul_high(row_inputs, w_key)).reshape(row_length, H, HD)
    value_rows = low(low_back(matmul_high(row_inputs, w_value))).reshape(row_length, H, HD)
    cos_table, sin_table = rope_tables(positions_of(segment_row))
    queries = low(rotate(rms_norm(queries, norm_query.reshape(H, HD)), cos_table, sin_table))
    key_rows = low(rotate(rms_norm(key_rows, norm_key.reshape(H, HD)), cos_table, sin_table))
    scores = low_back(jnp.einsum('ihd,jhd->hij', queries, key_rows, precision=HIGH) / math.sqrt(HD))
    position = jnp.arange(row_length, dtype=jnp.int32)
    allowed = (segment_row[:, None] == segment_row[None, :]) & (position[None, :] <= position[:, None])
    scores = jnp.where(allowed[None], scores, -1e+30)
    weights = low(jax.nn.softmax(scores, axis=-1))
    attended = jnp.einsum('hij,jhd->ihd', weights, value_rows, precision=HIGH).reshape(row_length, MODEL_DIM)
    attended = low(low_back(attended))
    return low_back(matmul_high(attended, w_output))

def slot_owner(routes):
    device_count = N_EXP * N_TP
    assigned = routes.reshape(device_count, TOK_DEV * TOP)
    matches = (assigned[:, :, None] == jnp.arange(EXPERTS, dtype=jnp.int32)[None, None, :]).astype(jnp.int32)
    earlier = (lax.optimization_barrier(jnp.sum(jnp.cumsum(matches, axis=1) * matches, axis=2)) - 1).astype(jnp.int32)
    device_ids = jnp.arange(device_count, dtype=jnp.int32)[:, None]
    slot_ids = jnp.where(earlier < CAP, assigned * (device_count * CAP) + device_ids * CAP + earlier, EXPERTS * device_count * CAP).astype(jnp.int32)
    owners = jnp.full((EXPERTS * device_count * CAP + 1,), TOTAL_TOKENS * TOP, jnp.int32)
    owners = owners.at[slot_ids.reshape(-1)].set(jnp.arange(TOTAL_TOKENS * TOP, dtype=jnp.int32))
    return owners[:-1].reshape(EXPERTS, device_count * CAP)

def run_expert(input_pad, gate_pad, assign_ids, w_gate, w_up, w_down):
    token_ids = assign_ids // TOP
    inputs = low_back(input_pad[token_ids])
    span_width = FF_E // N_TP
    summed = jnp.zeros((inputs.shape[0], MODEL_DIM), jnp.float32)
    for portion in range(N_TP):
        lower_col = portion * span_width
        upper_col = lower_col + span_width
        part_inputs = low_back(inputs)
        gate_part = low_back(matmul_high(part_inputs, w_gate[:, lower_col:upper_col]))
        up_part = low_back(matmul_high(part_inputs, w_up[:, lower_col:upper_col]))
        hidden = low(jax.nn.silu(gate_part) * up_part)
        summed = summed + low(matmul_high(hidden, w_down[lower_col:upper_col]))
    returned = low(low_back(summed))
    return (token_ids, gate_pad[assign_ids][:, None] * returned)

def reference(tokens, cotangent, attention_gain, query_weight, key_weight, value_weight, output_weight, query_norm, key_norm, mixture_gain, router_weight, gate_weight, up_weight, down_weight, routes, segments):
    owners = slot_owner(routes)

    def forward(inputs, gain_one, w_query, w_key, w_value, w_output, norm_query, norm_key, gain_two, w_router, w_gate, w_up, w_down):
        normalized_input = low(rms_norm(inputs, gain_one))

        def attend_documents(row_item):
            return attend_row(row_item[0], row_item[1], w_query, w_key, w_value, w_output, norm_query, norm_key)
        attention_block = lax.map(jax.checkpoint(attend_documents), (normalized_input.reshape(PACKED_ROWS, PACKED_LENGTH, MODEL_DIM), segments)).reshape(TOTAL_TOKENS, MODEL_DIM)
        middle = inputs + attention_block
        mixture_in = low(rms_norm(middle, gain_two))
        probabilities = jax.nn.softmax(matmul_high(mixture_in, w_router), axis=-1)
        gate_values = jnp.take_along_axis(probabilities, routes, axis=1)
        gate_pad = jnp.concatenate([gate_values.reshape(-1), jnp.zeros((1,), jnp.float32)])
        input_pad = jnp.concatenate([mixture_in, jnp.zeros((1, MODEL_DIM), jnp.float32)], axis=0)

        def expert_step(carried, pieces):
            token_ids, contrib = run_expert(input_pad, gate_pad, pieces[0], pieces[1], pieces[2], pieces[3])
            return (carried.at[token_ids].add(contrib), None)
        mixture, _ = lax.scan(jax.checkpoint(expert_step), jnp.zeros((TOTAL_TOKENS + 1, MODEL_DIM), jnp.float32), (owners, w_gate, w_up, w_down))
        return middle + mixture[:TOTAL_TOKENS]
    floats = (tokens.astype(jnp.float32), attention_gain.astype(jnp.float32), query_weight.astype(jnp.float32), key_weight.astype(jnp.float32), value_weight.astype(jnp.float32), output_weight.astype(jnp.float32), query_norm.astype(jnp.float32), key_norm.astype(jnp.float32), mixture_gain.astype(jnp.float32), router_weight.astype(jnp.float32), gate_weight.astype(jnp.float32), up_weight.astype(jnp.float32), down_weight.astype(jnp.float32))
    output, pullback = jax.vjp(forward, *floats)
    gradients = pullback(cotangent.astype(jnp.float32))
    return (output.astype(jnp.bfloat16), gradients[0], gradients[1], gradients[2], gradients[3], gradients[4], gradients[5], gradients[6], gradients[7], gradients[8], gradients[9], gradients[10], gradients[11], gradients[12])
```

```python
import functools
import math

import jax
import jax.numpy as jnp
from jax import lax
from jax.experimental import pallas as pl
from jax.experimental.pallas import tpu as pltpu
from jax.sharding import PartitionSpec as P

HD = 128


EPS = 1e-05
HIGH = lax.Precision.HIGHEST


def inverse_rms(values):
    return lax.rsqrt(jnp.mean(values * values, axis=-1, keepdims=True) + EPS)


def norm_backward(grad_normed, normalized_input, factor):
    return factor * (
        grad_normed
        - normalized_input * jnp.mean(grad_normed * normalized_input, axis=-1, keepdims=True)
    )


def contract_rows(first_arg, second_arg):
    return lax.dot_general(
        first_arg, second_arg, (((0,), (0,)), ((), ())), preferred_element_type=jnp.float32
    )


def contract_cols(first_arg, second_arg):
    return lax.dot_general(
        first_arg, second_arg, (((1,), (1,)), ((), ())), preferred_element_type=jnp.float32
    )


def positions_of(segment_row):
    earlier = jnp.sum((segment_row[None, :] < segment_row[:, None]).astype(jnp.int32), axis=1)
    return jnp.arange(segment_row.shape[0], dtype=jnp.int32) - earlier


def rope_tables(positions):
    half_dim = HD // 2
    inverse_freq = 10000.0 ** (-2.0 * jnp.arange(half_dim).astype(jnp.float32) / HD)
    angles = positions.astype(jnp.float32)[:, None] * inverse_freq[None, :]
    cos, sin = jnp.cos(angles), jnp.sin(angles)
    return jnp.concatenate([cos, cos], axis=1), jnp.concatenate([-sin, sin], axis=1)


def rotate(values, cos_table, sin_table):
    return values * cos_table + pltpu.roll(values, HD // 2, 1) * sin_table


def masked_scores(query_rot, key_rot, info):
    scores = contract_cols(query_rot, key_rot) * (1.0 / math.sqrt(HD))
    seg_col, row_col, seg_row, row_row = info
    allowed = (seg_col == seg_row) & (row_row <= row_col)
    return jnp.where(allowed, scores, -1e30)


def attend_kernel(
    rows_ref,
    query_weight,
    key_weight,
    value_weight,
    query_norm,
    key_norm,
    cos_ref,
    sin_ref,
    seg_col,
    row_col,
    seg_row,
    row_row,
    query_ref,
    key_ref,
    query_rot_ref,
    key_rot_ref,
    value_ref,
    attended_ref,
    total_ref,
):
    rows = rows_ref[...]
    cos_table, sin_table = cos_ref[...], sin_ref[...]
    info = (seg_col[...], row_col[...], seg_row[...], row_row[...])
    query_ref[...] = jnp.dot(rows, query_weight[...], preferred_element_type=jnp.float32)
    key_ref[...] = jnp.dot(rows, key_weight[...], preferred_element_type=jnp.float32)
    value_ref[...] = jnp.dot(
        rows, value_weight[...], preferred_element_type=jnp.float32
    ).astype(jnp.bfloat16)
    for head in range(query_ref.shape[1] // HD):
        span = slice(head * HD, (head + 1) * HD)
        queries, keys = query_ref[:, span], key_ref[:, span]
        query_rot = rotate(
            queries * inverse_rms(queries) * query_norm[:, span], cos_table, sin_table
        ).astype(jnp.bfloat16)
        key_rot = rotate(
            keys * inverse_rms(keys) * key_norm[:, span], cos_table, sin_table
        ).astype(jnp.bfloat16)
        query_rot_ref[:, span] = query_rot
        key_rot_ref[:, span] = key_rot
        scores = masked_scores(query_rot, key_rot, info)
        peak = jnp.max(scores, axis=-1, keepdims=True)
        shifted = jnp.exp(scores - peak)
        denominator = jnp.sum(shifted, axis=-1, keepdims=True)
        weights = (shifted / denominator).astype(jnp.bfloat16)
        attended_ref[:, span] = jnp.dot(
            weights, value_ref[:, span], preferred_element_type=jnp.float32
        ).astype(jnp.bfloat16)
        total_ref[head] = peak + jnp.log(denominator)


def attend_back_kernel(
    which_ref,
    row_grad_ref,
    output_weight,
    query_ref,
    key_ref,
    query_rot_ref,
    key_rot_ref,
    value_ref,
    total_ref,
    query_norm,
    key_norm,
    cos_ref,
    sin_ref,
    seg_col,
    row_col,
    seg_row,
    row_row,
    grad_query_ref,
    grad_key_ref,
    grad_value_ref,
    query_norm_grad,
    key_norm_grad,
):
    cos_table, sin_table = cos_ref[...], -sin_ref[...]
    info = (seg_col[...], row_col[...], seg_row[...], row_row[...])
    inv_sqrt = 1.0 / math.sqrt(HD)
    grad_attended = contract_cols(row_grad_ref[...], output_weight[...]).astype(jnp.bfloat16)

    def finish(grad_rot, raw, gain, out_ref, gain_ref, span):
        grad_norm = rotate(grad_rot, cos_table, sin_table)
        scale = inverse_rms(raw)
        hat = raw * scale
        gain_ref[:, span] = jnp.sum(grad_norm * hat, axis=0, keepdims=True)
        out_ref[:, span] = norm_backward(grad_norm * gain, hat, scale).astype(jnp.bfloat16)

    for head in range(query_ref.shape[1] // HD):
        span = slice(head * HD, (head + 1) * HD)
        query_rot, key_rot = query_rot_ref[:, span], key_rot_ref[:, span]
        grad_head = grad_attended[:, span]
        probs = jnp.exp(masked_scores(query_rot, key_rot, info) - total_ref[head])
        grad_weights = contract_cols(grad_head, value_ref[:, span])
        inner = jnp.sum(grad_weights * probs, axis=-1, keepdims=True)
        grad_scores = (probs * (grad_weights - inner)).astype(jnp.bfloat16)
        grad_value_ref[:, span] = contract_rows(probs.astype(jnp.bfloat16), grad_head).astype(
            jnp.bfloat16
        )
        grad_query_rot = (
            jnp.dot(grad_scores, key_rot, preferred_element_type=jnp.float32) * inv_sqrt
        )
        grad_key_rot = contract_rows(grad_scores, query_rot) * inv_sqrt
        finish(
            grad_query_rot,
            query_ref[:, span],
            query_norm[:, span],
            grad_query_ref,
            query_norm_grad,
            span,
        )
        finish(
            grad_key_rot, key_ref[:, span], key_norm[:, span], grad_key_ref, key_norm_grad, span
        )


def head_specs(length, width, model_width, wide):
    whole = pl.BlockSpec((length, model_width), lambda i: (0, 0))
    across = pl.BlockSpec((model_width, wide), lambda i: (0, i))
    down = pl.BlockSpec((wide, model_width), lambda i: (i, 0))
    heads = pl.BlockSpec((length, wide), lambda i: (0, i))
    gain = pl.BlockSpec((1, wide), lambda i: (0, i))
    total = pl.BlockSpec((wide // HD, length, 1), lambda i: (i, 0, 0))
    table = pl.BlockSpec((length, HD), lambda i: (0, 0))
    col = pl.BlockSpec((length, 1), lambda i: (0, 0))
    row = pl.BlockSpec((1, length), lambda i: (0, 0))
    return whole, across, down, heads, gain, total, [table, table, col, col, row, row]


def attend(rows, weights, gains, tables):
    length, model_width = rows.shape
    width = weights[0].shape[1]
    wide = min(2 * HD, width)
    whole, across, _, heads, gain, total, table_specs = head_specs(
        length, width, model_width, wide
    )
    low = jnp.bfloat16
    types = [jnp.float32, jnp.float32, low, low, low, low]
    return pl.pallas_call(
        attend_kernel,
        grid=(width // wide,),
        in_specs=[whole, across, across, across, gain, gain] + table_specs,
        out_specs=[heads] * 6 + [total],
        out_shape=[jax.ShapeDtypeStruct((length, width), t) for t in types]
        + [jax.ShapeDtypeStruct((width // HD, length, 1), jnp.float32)],
        cost_estimate=pl.CostEstimate(
            flops=6 * length * width * (model_width + length),
            bytes_accessed=2 * model_width * (length + 3 * width),
            transcendentals=width // HD * length * length,
        ),
        name="attend",
    )(rows, *weights, *gains, *tables)


def attend_back(which, row_grad, output_weight, saved, gains, tables, wide):
    length, model_width = row_grad.shape
    low = jnp.bfloat16
    whole = pl.BlockSpec((length, model_width), lambda i, w: (0, 0))
    down = pl.BlockSpec((wide, model_width), lambda i, w: (w[0], 0))
    heads = pl.BlockSpec((length, wide), lambda i, w: (0, w[0]))
    gain = pl.BlockSpec((1, wide), lambda i, w: (0, w[0]))
    total = pl.BlockSpec((wide // HD, length, 1), lambda i, w: (w[0], 0, 0))
    table = pl.BlockSpec((length, HD), lambda i, w: (0, 0))
    col = pl.BlockSpec((length, 1), lambda i, w: (0, 0))
    row = pl.BlockSpec((1, length), lambda i, w: (0, 0))
    out = pl.BlockSpec((length, wide), lambda i, w: (0, 0))
    gain_out = pl.BlockSpec((1, wide), lambda i, w: (0, 0))
    return pl.pallas_call(
        attend_back_kernel,
        grid_spec=pltpu.PrefetchScalarGridSpec(
            num_scalar_prefetch=1,
            grid=(1,),
            in_specs=[whole, down]
            + [heads] * 5
            + [total, gain, gain, table, table, col, col, row, row],
            out_specs=[out] * 3 + [gain_out] * 2,
        ),
        out_shape=[jax.ShapeDtypeStruct((length, wide), low)] * 3
        + [jax.ShapeDtypeStruct((1, wide), jnp.float32)] * 2,
        cost_estimate=pl.CostEstimate(
            flops=2 * length * wide * (model_width + 5 * length),
            bytes_accessed=2 * model_width * (length + wide) + 16 * length * wide,
            transcendentals=wide // HD * length * length,
        ),
        name="attend_back",
    )(which, row_grad, output_weight, *saved, *gains, *tables)


AXES = ("exp", "tp")


def after(value, others):
    return lax.optimization_barrier((value, others))[0]


class Links:
    def __init__(self, n_exp, n_tp):
        self.n_exp, self.n_tp, self.n_z = n_exp, n_tp, n_exp // 2

    def send(self, value, place):
        pairs = []
        for z in range(self.n_z):
            for x in range(2):
                for y in range(2):
                    for c in range(2):
                        z2, x2, y2, c2 = place(z, x, y, c)
                        pairs.append(((z * 2 + x) * 4 + y * 2 + c, (z2 * 2 + x2) * 4 + y2 * 2 + c2))
        return lax.ppermute(value, AXES, pairs)

    def core(self, value):
        return self.send(value, lambda z, x, y, c: (z, x, y, 1 - c))

    def flip_x(self, value):
        return self.send(value, lambda z, x, y, c: (z, 1 - x, y, c))

    def flip_y(self, value):
        return self.send(value, lambda z, x, y, c: (z, x, 1 - y, c))

    def first(self, value):
        return self.send(value, lambda z, x, y, c: (z, x ^ (1 - c), y ^ c, c))

    def second(self, value):
        return self.send(value, lambda z, x, y, c: (z, x ^ c, y ^ (1 - c), c))

    def along_z(self, value, steps):
        return self.send(value, lambda z, x, y, c: ((z + steps) % self.n_z, x, y, c))

    def flip_z(self, value, bit):
        return self.send(value, lambda z, x, y, c: (z ^ bit, x, y, c))

    def spread(self, block, axis=0):
        near = jnp.concatenate([block, self.first(block)], axis=axis)
        plane = jnp.concatenate([near, self.second(near)], axis=axis)
        return plane, self.core(plane)

    def collect(self, plane, partner, kind):
        total = plane.astype(jnp.float32) + self.core(partner.astype(kind)).astype(jnp.float32)
        half = total.shape[0] // 2
        total = total[:half] + self.second(total[half:].astype(kind)).astype(jnp.float32)
        half = half // 2
        return total[:half] + self.first(total[half:].astype(kind)).astype(jnp.float32)

    def tp_rows(self, block):
        far = self.flip_y(block)
        return jnp.concatenate([block, self.core(block), far, self.core(far)], axis=0)

    def tp_sum(self, part):
        rows = part.shape[0] // 4
        sent = jnp.concatenate([part[rows : 2 * rows], part[3 * rows :]], axis=0)
        got = self.core(sent.astype(jnp.bfloat16)).astype(jnp.float32)
        far = part[2 * rows : 3 * rows] + got[rows:]
        return part[:rows] + got[:rows] + self.flip_y(far.astype(jnp.bfloat16)).astype(jnp.float32)

    def sum_exp(self, value):
        value = value + self.flip_x(value)
        for bit in range(self.n_z.bit_length() - 1):
            value = value + self.flip_z(value, 1 << bit)
        return value

    def sum_tp(self, value):
        value = value + self.core(value)
        return value + self.flip_y(value)


def gather_expert_rows(local_rows):
    return lax.all_gather(local_rows, "tp", axis=1, tiled=True)


def moe_slots(
    mixture_in, probabilities, grad_out, routes, capacity, gate_weight, up_weight, down_weight
):
    tok_rows, model_width = mixture_in.shape
    top_count = routes.shape[1]
    experts_all = probabilities.shape[1]
    expert_ids = jnp.arange(experts_all, dtype=jnp.int32)
    chosen = (routes[:, :, None] == expert_ids[None, None, :]).astype(jnp.float32)
    gate_values = jnp.sum(chosen * probabilities[:, None, :], axis=-1)
    assigned = routes.reshape(-1)
    matches = (assigned[:, None] == expert_ids[None, :]).astype(jnp.int32)
    earlier = jnp.sum(jnp.cumsum(matches, axis=0) * matches, axis=1) - 1
    slot_ids = jnp.where(earlier < capacity, assigned * capacity + earlier, experts_all * capacity)
    assign_count = tok_rows * top_count
    owners = (
        jnp.full((experts_all * capacity + 1,), assign_count, jnp.int32)
        .at[slot_ids]
        .set(jnp.arange(assign_count, dtype=jnp.int32))[:-1]
    )
    source_rows = owners // top_count
    input_pad = jnp.concatenate([mixture_in, jnp.zeros((1, model_width), jnp.bfloat16)], axis=0)
    outgoing = input_pad[source_rows].reshape(experts_all, capacity, model_width)
    arrived = lax.all_to_all(outgoing, "exp", split_axis=0, concat_axis=1, tiled=True)
    expert_in = gather_expert_rows(arrived)
    gate_pre = jnp.einsum(
        "erd,edf->erf", expert_in, gate_weight, preferred_element_type=jnp.float32
    )
    up_pre = jnp.einsum("erd,edf->erf", expert_in, up_weight, preferred_element_type=jnp.float32)
    hidden = (jax.nn.silu(gate_pre) * up_pre).astype(jnp.bfloat16)
    partial_out = jnp.einsum(
        "erf,efd->erd", hidden, down_weight, preferred_element_type=jnp.float32
    )
    returned = lax.psum_scatter(
        partial_out.astype(jnp.bfloat16), "tp", scatter_dimension=1, tiled=True
    )
    combined = lax.all_to_all(returned, "exp", split_axis=1, concat_axis=0, tiled=True)
    output_pad = jnp.concatenate(
        [combined.reshape(-1, model_width), jnp.zeros((1, model_width), jnp.bfloat16)], axis=0
    )
    expert_out = output_pad[slot_ids].astype(jnp.float32).reshape(tok_rows, top_count, model_width)
    mixture = jnp.sum(gate_values[:, :, None] * expert_out, axis=1)
    grad_gate = jnp.sum(grad_out[:, None, :] * expert_out, axis=-1)
    grad_sent = (
        (gate_values[:, :, None] * grad_out[:, None, :])
        .reshape(assign_count, model_width)
        .astype(jnp.bfloat16)
    )
    grad_pad = jnp.concatenate([grad_sent, jnp.zeros((1, model_width), jnp.bfloat16)], axis=0)
    grad_outgoing = grad_pad[owners].reshape(experts_all, capacity, model_width)
    grad_arrived = lax.all_to_all(grad_outgoing, "exp", split_axis=0, concat_axis=1, tiled=True)
    grad_expert = lax.all_gather(grad_arrived, "tp", axis=1, tiled=True)
    gate_pre = jnp.einsum(
        "erd,edf->erf", expert_in, gate_weight, preferred_element_type=jnp.float32
    )
    up_pre = jnp.einsum("erd,edf->erf", expert_in, up_weight, preferred_element_type=jnp.float32)
    gate_sig = jax.nn.sigmoid(gate_pre)
    gate_act = gate_pre * gate_sig
    hidden = (gate_act * up_pre).astype(jnp.bfloat16)
    grad_hidden = jnp.einsum(
        "erd,efd->erf", grad_expert, down_weight, preferred_element_type=jnp.float32
    )
    down_grad = jnp.einsum("erf,erd->efd", hidden, grad_expert, preferred_element_type=jnp.float32)
    grad_gate_pre = (grad_hidden * up_pre * gate_sig * (1.0 + gate_pre * (1.0 - gate_sig))).astype(
        jnp.bfloat16
    )
    grad_up_pre = (grad_hidden * gate_act).astype(jnp.bfloat16)
    gate_grad = jnp.einsum(
        "erd,erf->edf", expert_in, grad_gate_pre, preferred_element_type=jnp.float32
    )
    up_grad = jnp.einsum("erd,erf->edf", expert_in, grad_up_pre, preferred_element_type=jnp.float32)
    grad_in_part = jnp.einsum(
        "erf,edf->erd", grad_gate_pre, gate_weight, preferred_element_type=jnp.float32
    ) + jnp.einsum("erf,edf->erd", grad_up_pre, up_weight, preferred_element_type=jnp.float32)
    grad_in = lax.psum_scatter(
        grad_in_part.astype(jnp.bfloat16), "tp", scatter_dimension=1, tiled=True
    )
    grad_home = lax.all_to_all(grad_in, "exp", split_axis=1, concat_axis=0, tiled=True)
    home_pad = jnp.concatenate(
        [grad_home.reshape(-1, model_width), jnp.zeros((1, model_width), jnp.bfloat16)], axis=0
    )
    grad_assigned = home_pad[slot_ids].astype(jnp.float32).reshape(tok_rows, top_count, model_width)
    weighted = probabilities * jnp.sum(chosen * grad_gate[:, :, None], axis=1)
    return mixture, jnp.sum(grad_assigned, axis=1), weighted, gate_grad, up_grad, down_grad


def kept_experts(routes, experts_all, capacity):
    tok_rows = routes.shape[0]
    expert_ids = jnp.arange(experts_all, dtype=jnp.int32)
    member = jnp.sum((routes[:, :, None] == expert_ids[None, None, :]).astype(jnp.float32), axis=1)
    row = jnp.arange(tok_rows, dtype=jnp.int32)
    before = (row[None, :] < row[:, None]).astype(jnp.bfloat16)
    rank = jnp.dot(before, member.astype(jnp.bfloat16), preferred_element_type=jnp.float32)
    return jnp.where(rank < capacity, member, 0.0)


def expert_kernel(
    carried,
    tile,
    place,
    near_ref,
    far_ref,
    grad_near_ref,
    grad_far_ref,
    kept_ref,
    router_ref,
    gate_hbm,
    up_hbm,
    down_hbm,
    *refs,
):
    (
        mix_hbm,
        part_hbm,
        sum_ref,
        rows_all,
        grad_all,
        hidden_all,
        gate_all,
        up_all,
        rows,
        grads,
        gate_w,
        up_w,
        down_w,
        mix,
        part,
        hidden_v,
        gate_v,
        up_v,
        sem_in,
        sem_out,
    ) = refs[carried:]
    local_experts, _, hidden_width = gate_w.shape
    spans = [slice(e * hidden_width, (e + 1) * hidden_width) for e in range(local_experts)]
    loads = {}
    plan = [(("x", 0), near_ref, rows.at[0])]
    for e in range(local_experts):
        plan.append((("g", e), gate_hbm.at[e], gate_w.at[e]))
        plan.append((("u", e), up_hbm.at[e], up_w.at[e]))
        if e == 0:
            plan.append((("c", 0), grad_near_ref, grads.at[0]))
        plan.append((("d", e), down_hbm.at[spans[e], :], down_w.at[spans[e], :]))
    plan.append((("x", 1), far_ref, rows.at[1]))
    plan.append((("c", 1), grad_far_ref, grads.at[1]))
    for n, (key, source, target) in enumerate(plan):
        loads[key] = pltpu.make_async_copy(source, target, sem_in.at[n])
        loads[key].start()
    stores = []

    def store(source, target):
        copy = pltpu.make_async_copy(source, target, sem_out.at[len(stores)])
        copy.start()
        stores.append(copy)

    for t in range(2):
        at = pl.ds(place + t * tile, tile)
        loads["x", t].wait()
        store(rows.at[t], rows_all.at[at, :])
        x = rows[t]
        logits = jnp.dot(x, router_ref[...], preferred_element_type=jnp.float32)
        shifted = jnp.exp(logits - jnp.max(logits, axis=-1, keepdims=True))
        kept = kept_ref[t * tile : (t + 1) * tile, :]
        gates = shifted[:, :local_experts] / jnp.sum(shifted, axis=-1, keepdims=True) * kept
        sums = []
        total = None
        for e in range(local_experts):
            gate = gates[:, e : e + 1]
            if t == 0:
                loads["g", e].wait()
            gate_pre = jnp.dot(x, gate_w[e], preferred_element_type=jnp.float32)
            if t == 0:
                loads["u", e].wait()
            up_pre = jnp.dot(x, up_w[e], preferred_element_type=jnp.float32)
            if e == 0:
                loads["c", t].wait()
                store(grads.at[t], grad_all.at[at, :])
            if t == 0:
                loads["d", e].wait()
            back = contract_cols(grads[t], down_w[spans[e], :]) * gate
            sig = jax.nn.sigmoid(gate_pre)
            act = gate_pre * sig
            hidden = (act * up_pre).astype(jnp.bfloat16).astype(jnp.float32)
            sums.append(jnp.sum(hidden * back, axis=-1, keepdims=True))
            hidden_v[t, :, spans[e]] = (hidden * gate).astype(jnp.bfloat16)
            grad_gate = (back * up_pre * sig * (1.0 + gate_pre * (1.0 - sig))).astype(
                jnp.bfloat16
            )
            grad_up = (back * act).astype(jnp.bfloat16)
            gate_v[t, e] = grad_gate
            up_v[t, e] = grad_up
            piece = contract_cols(grad_gate, gate_w[e]) + contract_cols(grad_up, up_w[e])
            total = piece if total is None else total + piece
        part[t] = total.astype(jnp.bfloat16)
        store(part.at[t], part_hbm.at[pl.ds(t * tile, tile), :])
        for e in range(local_experts):
            store(gate_v.at[t, e], gate_all.at[e, at, :])
            store(up_v.at[t, e], up_all.at[e, at, :])
        store(hidden_v.at[t], hidden_all.at[at, :])
        sum_ref[t * tile : (t + 1) * tile, :] = jnp.concatenate(sums, axis=1)
        mix[t] = jnp.dot(
            hidden_v[t], down_w[...], preferred_element_type=jnp.float32
        ).astype(jnp.bfloat16)
        store(mix.at[t], mix_hbm.at[pl.ds(t * tile, tile), :])
    for copy in stores:
        copy.wait()


def run_experts(
    place, count, rows, grads, kept, router, gate_weight, up_weight, down_flat, carried
):
    tile, model_width = rows[0].shape
    local_experts, _, hidden_width = gate_weight.shape
    flat = local_experts * hidden_width
    tok_count = 2 * tile
    whole = tok_count * count
    low = jnp.bfloat16
    hbm = pl.BlockSpec(memory_space=pl.ANY)
    vmem = pl.BlockSpec(memory_space=pltpu.VMEM)
    out = pl.pallas_call(
        functools.partial(expert_kernel, len(carried), tile, place * tok_count),
        in_specs=[hbm] * 4 + [vmem] * 2 + [hbm] * (3 + len(carried)),
        out_specs=[hbm, hbm, vmem] + [hbm] * 5,
        out_shape=[
            jax.ShapeDtypeStruct((tok_count, model_width), low),
            jax.ShapeDtypeStruct((tok_count, model_width), low),
            jax.ShapeDtypeStruct((tok_count, local_experts), jnp.float32),
            jax.ShapeDtypeStruct((whole, model_width), low),
            jax.ShapeDtypeStruct((whole, model_width), low),
            jax.ShapeDtypeStruct((whole, flat), low),
            jax.ShapeDtypeStruct((local_experts, whole, hidden_width), low),
            jax.ShapeDtypeStruct((local_experts, whole, hidden_width), low),
        ],
        scratch_shapes=[
            pltpu.VMEM((2, tile, model_width), low),
            pltpu.VMEM((2, tile, model_width), low),
            pltpu.VMEM(gate_weight.shape, low),
            pltpu.VMEM(up_weight.shape, low),
            pltpu.VMEM(down_flat.shape, low),
            pltpu.VMEM((2, tile, model_width), low),
            pltpu.VMEM((2, tile, model_width), low),
            pltpu.VMEM((2, tile, flat), low),
            pltpu.VMEM((2, local_experts, tile, hidden_width), low),
            pltpu.VMEM((2, local_experts, tile, hidden_width), low),
            pltpu.SemaphoreType.DMA((4 + 3 * local_experts,)),
            pltpu.SemaphoreType.DMA((2 * (5 + 2 * local_experts),)),
        ],
        input_output_aliases={9 + i: 3 + i for i in range(len(carried))},
        cost_estimate=pl.CostEstimate(
            flops=16 * tok_count * model_width * flat,
            bytes_accessed=12 * model_width * (tok_count + flat),
            transcendentals=tok_count * flat,
        ),
        name="experts",
    )(*rows, *grads, kept, router, gate_weight, up_weight, down_flat, *carried)
    return out[:3], list(out[3:])


class HalfSum:
    def __init__(self, links, value):
        self.links, self.value = links, value
        self.bits = [1 << b for b in range(links.n_z.bit_length() - 1)]

    def stages(self):
        return 2 * len(self.bits)

    def go(self, stage, ties=()):
        links, value, count = self.links, self.value, len(self.bits)
        z = lax.axis_index("exp") // 2
        if stage < count:
            bit = self.bits[stage]
            upper = (z // bit) % 2
            half = value.shape[0] // 2
            kept = lax.dynamic_slice_in_dim(value, upper * half, half, axis=0)
            sent = lax.dynamic_slice_in_dim(value, (1 - upper) * half, half, axis=0)
            got = links.flip_z(after(sent.astype(jnp.bfloat16), ties), bit)
            value = kept + got.astype(jnp.float32)
            if stage == count - 1:
                value = value.astype(jnp.bfloat16)
        else:
            bit = self.bits[2 * count - 1 - stage]
            got = links.flip_z(after(value, ties), bit)
            value = jnp.where(
                (z // bit) % 2 == 0,
                jnp.concatenate([value, got], axis=0),
                jnp.concatenate([got, value], axis=0),
            )
        self.value = value
        return got


class Spread:
    def __init__(self, links, block, order):
        self.links, self.order = links, order
        self.blocks, self.near, self.far, self.other = {0: block}, {}, {}, {}

    def go_z(self, k, ties=()):
        self.blocks[k] = self.links.along_z(after(self.blocks[0], ties), self.order[k])
        return self.blocks[k]

    def go_near(self, k, ties=()):
        block = after(self.blocks[k], ties)
        self.near[k] = jnp.concatenate([block, self.links.first(block)], axis=0)
        return self.near[k]

    def go_far(self, k, ties=()):
        self.far[k] = self.links.second(after(self.near[k], ties))
        return self.far[k]

    def go_core(self, k, ties=()):
        near, far = after((self.near[k], self.far[k]), ties)
        self.other[k] = (self.links.core(near), self.links.core(far))
        return self.other[k]

    def plane(self, k, side):
        return self.other[k] if side else (self.near[k], self.far[k])


class Gathering:
    def __init__(self, links, order):
        self.links, self.order, self.terms = links, order, {}

    def total(self, k, first, last):
        wide = [t[first:last].astype(jnp.float32) for t in self.terms[k]]
        return functools.reduce(jnp.add, wide)

    def go_core(self, k, own, partner, ties=()):
        self.terms[k] = [own, self.links.core(after(partner, ties))]
        return self.terms[k][-1]

    def go_second(self, k, ties=()):
        rows = self.terms[k][0].shape[0]
        sent = self.total(k, rows // 2, rows).astype(jnp.bfloat16)
        self.terms[k].append(self.links.second(after(sent, ties)))
        return self.terms[k][-1]

    def go_first(self, k, ties=()):
        rows = self.terms[k][0].shape[0]
        sent = self.total(k, rows // 4, rows // 2).astype(jnp.bfloat16)
        self.terms[k].append(self.links.first(after(sent, ties)))
        return self.terms[k][-1]

    def go_z(self, k, ties=()):
        rows = self.terms[k][0].shape[0]
        sent = self.total(k, 0, rows // 4)
        if k:
            sent = self.links.along_z(after(sent.astype(jnp.bfloat16), ties), -self.order[k])
        self.terms[k] = [sent]
        return sent

    def home(self):
        return functools.reduce(
            jnp.add, [self.terms[k][0].astype(jnp.float32) for k in range(len(self.order))]
        )


def moe_dense(
    links,
    order,
    attention_in,
    mixture_in,
    grads,
    kept_chunks,
    router_weight,
    gate_weight,
    up_weight,
    down_weight,
):
    tok_rows, model_width = mixture_in.shape
    local_experts, _, hidden_width = gate_weight.shape
    experts_all = router_weight.shape[1]
    first_expert = lax.axis_index("exp") * local_experts
    down_flat = down_weight.reshape(local_experts * hidden_width, model_width)
    router = jnp.roll(router_weight, -first_expert, axis=1)
    n_z = links.n_z
    kept_own = [
        [lax.dynamic_slice_in_dim(k, first_expert, local_experts, axis=1) for k in kept_chunks[r]]
        for r in order
    ]
    rows = Spread(links, mixture_in, order)
    back = Gathering(links, order)
    mix = Gathering(links, order)
    carried = []
    own, partner = [None] * n_z, [None] * n_z

    def experts(k, side, ties):
        nonlocal carried
        result, carried = run_experts(
            2 * k + side,
            2 * n_z,
            rows.plane(k, side),
            grads.plane(k, side),
            after(kept_own[k][side], ties),
            router,
            gate_weight,
            up_weight,
            down_flat,
            carried,
        )
        return result

    rows.go_near(0)
    rows.go_z(1)
    grads.go_core(0)
    grads.go_core(1)
    rows.go_far(0)
    held = [grads.go_near(2)]
    for k in range(n_z):
        own[k] = experts(k, 0, held)
        held = [rows.go_core(k)]
        if k + 1 < n_z:
            held.append(rows.go_near(k + 1))
        if k + 2 < n_z:
            held.append(rows.go_z(k + 2, [rows.blocks[k + 1]]))
            if k == 0:
                held.append(grads.go_far(2))
                grads.go_core(2)
            elif k == 1:
                held.append(grads.go_far(3))
                grads.go_core(3)
        if k >= 2:
            held.append(back.go_first(k - 2))
        if k >= 1:
            held.append(back.go_core(k - 1, own[k - 1][1], partner[k - 1][1]))
        partner[k] = experts(k, 1, held)
        held = []
        if k + 1 < n_z:
            rows.go_far(k + 1)
        if k == 0:
            held.append(grads.go_near(3))
        if k >= 2:
            held.append(back.go_z(k - 2))
        if k >= 1:
            held.append(back.go_second(k - 1))
    step_one = [
        back.go_core(n_z - 1, own[n_z - 1][1], partner[n_z - 1][1]),
        back.go_first(n_z - 2),
    ]
    rows_all, grad_all, hidden_all, gate_all, up_all = carried
    step_two = [
        back.go_second(n_z - 1),
        back.go_z(n_z - 2),
        mix.go_core(0, own[0][0], partner[0][0], step_one),
        mix.go_core(1, own[1][0], partner[1][0], step_one),
    ]
    gate_all = after(gate_all, step_one)
    gate_grad = jnp.stack([contract_rows(rows_all, gate_all[e]) for e in range(local_experts)])
    step_three = [
        back.go_first(n_z - 1),
        mix.go_core(2, own[2][0], partner[2][0], step_two),
        mix.go_core(3, own[3][0], partner[3][0], step_two),
    ]
    up_all = after(up_all, step_two)
    up_grad = jnp.stack([contract_rows(rows_all, up_all[e]) for e in range(local_experts)])
    back.go_z(n_z - 1)
    early_x = links.flip_x(after(attention_in, step_three))
    mix.go_second(0, [early_x])
    hidden_all = after(hidden_all, step_three)
    down_grad = contract_rows(hidden_all, grad_all).reshape(
        local_experts, hidden_width, model_width
    )
    full = []
    for parts in (own, partner):
        planes = []
        for k in range(n_z):
            local = parts[k][2].reshape(-1, tok_rows, local_experts).transpose(0, 2, 1)
            zero = jnp.zeros((local.shape[0], experts_all, tok_rows), jnp.float32)
            planes.append(lax.dynamic_update_slice_in_dim(zero, local, first_expert, axis=1))
        full.append(jnp.stack(planes, axis=1))
    small = links.collect(full[0], full[1], jnp.float32)[0]
    weighted = small[0]
    for k in range(1, n_z):
        weighted = weighted + links.along_z(small[k], -order[k])
    input_grad = after(back.home(), [mix.terms[0][-1]])
    return mix, early_x, input_grad, weighted.T, gate_grad, up_grad, down_grad


def body(
    mesh_sizes,
    tokens,
    cotangent,
    attention_gain,
    query_weight,
    key_weight,
    value_weight,
    output_weight,
    query_norm,
    key_norm,
    mixture_gain,
    router_weight,
    gate_weight,
    up_weight,
    down_weight,
    routes,
    segments,
):
    tok_rows, model_width = tokens.shape
    top_count = routes.shape[1]
    experts_all = router_weight.shape[1]
    capacity = tok_rows * top_count * 7 // (8 * experts_all)
    local_width = query_weight.shape[1]
    n_exp, n_tp = mesh_sizes
    dense = experts_all <= 2 * top_count and n_tp == 4 and n_exp % 2 == 0
    links = Links(n_exp, n_tp)
    grad_out = cotangent.astype(jnp.float32)
    if dense:
        kept = kept_experts(routes, experts_all, capacity).T.astype(jnp.bfloat16)
        kept_z = jnp.stack([kept] + [links.along_z(kept, r) for r in range(1, n_exp // 2)])
        kept_planes = links.spread(kept_z[None])
        kept_chunks = [
            [
                plane[:, r].transpose(0, 2, 1).reshape(-1, experts_all).astype(jnp.float32)
                for plane in kept_planes
            ]
            for r in range(n_exp // 2)
        ]
        order = [0, 1, 3, 2] if n_exp == 8 else list(range(n_exp // 2))
        grads = Spread(links, cotangent, order)
        held = [grads.go_near(0), grads.go_z(1)]
    else:
        held = []
    inputs = tokens.astype(jnp.float32)
    scale_one = inverse_rms(inputs)
    normed_one = inputs * scale_one
    attention_in = (normed_one * attention_gain).astype(jnp.bfloat16)
    segment_row = segments[0]
    tp_order = lax.axis_index("tp") ^ jnp.arange(n_tp, dtype=jnp.int32)
    positions = positions_of(segment_row).reshape(n_tp, tok_rows)[tp_order].reshape(-1)
    segment_rel = segment_row.reshape(n_tp, tok_rows)[tp_order].reshape(-1)
    row_rel = (
        tp_order[:, None] * tok_rows + jnp.arange(tok_rows, dtype=jnp.int32)[None, :]
    ).reshape(-1)
    tables = (
        *rope_tables(positions),
        segment_rel[:, None],
        row_rel[:, None],
        segment_rel[None, :],
        row_rel[None, :],
    )
    gains = (query_norm[None, :], key_norm[None, :])
    gathered_rows = links.tp_rows(attention_in)
    rows_held = after(gathered_rows, held)
    if dense:
        held = [
            grads.go_far(0, [gathered_rows]),
            grads.go_near(1, [grads.far[0]]),
            grads.go_z(2, [grads.blocks[1]]),
        ]
    *saved, attended, log_totals = attend(
        rows_held, (query_weight, key_weight, value_weight), gains, tables
    )
    partial_block = jnp.dot(after(attended, held), output_weight, preferred_element_type=jnp.float32)
    held = [grads.go_far(1), grads.go_z(3, [grads.blocks[2]])] if dense else []
    attention_block = after(links.tp_sum(partial_block), held)
    middle = inputs + attention_block
    scale_two = inverse_rms(middle)
    normed_two = middle * scale_two
    mixture_in = (normed_two * mixture_gain).astype(jnp.bfloat16)
    logits = jnp.dot(mixture_in, router_weight, preferred_element_type=jnp.float32)
    probabilities = jax.nn.softmax(logits, axis=-1)
    if dense:
        mix, early_x, grad_expert_in, weighted, gate_grad, up_grad, down_grad = moe_dense(
            links,
            order,
            attention_in,
            mixture_in,
            grads,
            kept_chunks,
            router_weight,
            gate_weight,
            up_weight,
            down_weight,
        )
    else:
        mixture, grad_expert_in, weighted, gate_grad, up_grad, down_grad = moe_slots(
            mixture_in,
            probabilities,
            grad_out,
            routes,
            capacity,
            gate_weight,
            up_weight,
            down_weight,
        )
        early_x = links.flip_x(attention_in)
    grad_logits = weighted - probabilities * jnp.sum(weighted, axis=-1, keepdims=True)
    router_grad = jnp.dot(mixture_in.astype(jnp.float32).T, grad_logits, precision=HIGH)
    grad_mixture_in = grad_expert_in + jnp.dot(
        grad_logits, router_weight.astype(jnp.float32).T, precision=HIGH
    )
    mixture_gain_grad = jnp.sum(grad_mixture_in * normed_two, axis=0)
    grad_middle = grad_out + norm_backward(grad_mixture_in * mixture_gain, normed_two, scale_two)
    grad_attention = grad_middle.astype(jnp.bfloat16)
    row_grad = links.tp_rows(grad_attention)
    wide = local_width // 2
    side = lax.axis_index("exp") % 2
    peer_attention = links.flip_x(grad_attention)
    attended_other = lax.dynamic_slice_in_dim(attended, (1 - side) * wide, wide, axis=1)
    peer_rows = links.tp_rows(after(early_x, row_grad))
    held = [peer_attention, peer_rows]
    if dense:
        held.append(mix.go_first(0))
    results = [None, None]
    for turn in range(2):
        which = 1 - side if turn == 0 else side
        ties = [r[0] for r in results[:turn]]
        if turn == 1:
            ties += held
        results[turn] = attend_back(
            after(which.astype(jnp.int32)[None], ties),
            row_grad,
            output_weight,
            (*saved, log_totals),
            gains,
            tables,
            wide,
        )
    other = jnp.concatenate(results[0][:3], axis=1)
    peer_grads = links.flip_x(after(other, held))
    attended_peer = links.flip_x(after(attended_other, held))
    peer_row_grad = links.tp_rows(after(peer_attention, held))
    own_grads = jnp.concatenate(results[1][:3], axis=1)

    def in_order(own_part, other_part, axis):
        return jnp.where(
            side == 0,
            jnp.concatenate([own_part, other_part], axis=axis),
            jnp.concatenate([other_part, own_part], axis=axis),
        )

    grad_queries, grad_keys, grad_values, query_norm_grad, key_norm_grad = [
        in_order(results[1][i], results[0][i], 1) for i in range(5)
    ]
    query_norm_grad, key_norm_grad = query_norm_grad[0], key_norm_grad[0]
    total_grad = contract_cols(grad_queries, query_weight)
    total_grad = total_grad + contract_cols(grad_keys, key_weight)
    total_grad = total_grad + contract_cols(grad_values, value_weight)
    held = [peer_row_grad, attended_peer]
    grad_attention_in = links.tp_sum(after(total_grad, held))
    attended_own = lax.dynamic_slice_in_dim(attended, side * wide, wide, axis=1)
    own_parts = [attended_own] + [gathered_rows] * 3
    peer_parts = [attended_peer] + [peer_rows] * 3
    own_ends = [row_grad] + [own_grads[:, i * wide : (i + 1) * wide] for i in range(3)]
    peer_ends = [peer_row_grad] + [peer_grads[:, i * wide : (i + 1) * wide] for i in range(3)]
    pieces = [
        HalfSum(links, contract_rows(p, q) + contract_rows(r, s))
        for p, q, r, s in zip(own_parts, own_ends, peer_parts, peer_ends)
    ]
    stages = pieces[0].stages()
    big_sums = [None] * 4
    if dense:
        mix_steps = (
            [lambda t, k=k: mix.go_second(k, t) for k in range(1, links.n_z)]
            + [lambda t, k=k: mix.go_first(k, t) for k in range(1, links.n_z)]
            + [lambda t, k=k: mix.go_z(k, t) for k in range(links.n_z)]
        )
    else:
        mix_steps = []
    last = [None] * stages
    ties = []
    for step in range(stages + 4):
        moved = []
        for p in range(4):
            stage = step - p
            if 0 <= stage < stages:
                moved.append(pieces[p].go(stage, ties))
            elif stage == stages:
                whole = pieces[p].value
                moved.append(links.flip_x(after(whole, ties)))
                big_sums[p] = (whole, moved[-1])
        for _ in range(2):
            if mix_steps:
                moved.append(mix_steps.pop(0)(ties))
        ties = moved
    big_sums = [
        in_order(whole, got, axis).astype(jnp.float32)
        for (whole, got), axis in zip(big_sums, (0, 1, 1, 1))
    ]
    output_weight_grad, query_weight_grad, key_weight_grad, value_weight_grad = big_sums
    if dense:
        while mix_steps:
            mix_steps.pop(0)([])
        mixture = mix.home()
    output = (middle + mixture).astype(jnp.bfloat16)
    attention_gain_grad = jnp.sum(grad_attention_in * normed_one, axis=0)
    tokens_grad = grad_middle + norm_backward(
        grad_attention_in * attention_gain, normed_one, scale_one
    )
    if dense:
        early = jnp.concatenate([mixture_gain_grad, router_grad.reshape(-1)])
        early = links.sum_tp(links.sum_exp(early))
        late = jnp.concatenate([query_norm_grad, key_norm_grad, attention_gain_grad])
        late = links.sum_exp(late)
        norm_sums = (late[:local_width], late[local_width : 2 * local_width])
        gain_sum = links.sum_tp(late[2 * local_width :])
        shared_sums = (
            gain_sum,
            early[:model_width],
            early[model_width:].reshape(model_width, experts_all),
        )
    else:
        norm_sums = [
            lax.psum(value.astype(jnp.bfloat16), "exp").astype(jnp.float32)
            for value in (query_norm_grad, key_norm_grad)
        ]
        shared_sums = lax.psum((attention_gain_grad, mixture_gain_grad, router_grad), AXES)
    return (
        output,
        tokens_grad,
        shared_sums[0],
        query_weight_grad,
        key_weight_grad,
        value_weight_grad,
        output_weight_grad,
        norm_sums[0],
        norm_sums[1],
        shared_sums[1],
        shared_sums[2],
        gate_grad,
        up_grad,
        down_grad,
    )


def solution(mesh):
    return jax.shard_map(
        functools.partial(body, (mesh.shape["exp"], mesh.shape["tp"])),
        mesh=mesh,
        in_specs=(
            P(("exp", "tp"), None),
            P(("exp", "tp"), None),
            P(),
            P(None, "tp"),
            P(None, "tp"),
            P(None, "tp"),
            P("tp", None),
            P("tp"),
            P("tp"),
            P(),
            P(),
            P("exp", None, "tp"),
            P("exp", None, "tp"),
            P("exp", "tp", None),
            P(("exp", "tp"), None),
            P("exp", None),
        ),
        out_specs=(
            P(("exp", "tp"), None),
            P(("exp", "tp"), None),
            P(),
            P(None, "tp"),
            P(None, "tp"),
            P(None, "tp"),
            P("tp", None),
            P("tp"),
            P("tp"),
            P(),
            P(),
            P("exp", None, "tp"),
            P("exp", None, "tp"),
            P("exp", "tp", None),
        ),
        check_vma=False,
    )
```

```python
import functools
import itertools
import math

import jax
import jax.numpy as jnp
from jax import lax
from jax.experimental import pallas as pl
from jax.experimental.pallas import tpu as pltpu
from jax.sharding import PartitionSpec as P

HD = 128


EPS = 1e-05
HIGH = lax.Precision.HIGHEST


def inverse_rms(values):
    return lax.rsqrt(jnp.mean(values * values, axis=-1, keepdims=True) + EPS)


def norm_backward(grad_normed, normalized_input, factor):
    return factor * (
        grad_normed
        - normalized_input * jnp.mean(grad_normed * normalized_input, axis=-1, keepdims=True)
    )


def contract_rows(first_arg, second_arg):
    return lax.dot_general(
        first_arg, second_arg, (((0,), (0,)), ((), ())), preferred_element_type=jnp.float32
    )


def contract_cols(first_arg, second_arg):
    return lax.dot_general(
        first_arg, second_arg, (((1,), (1,)), ((), ())), preferred_element_type=jnp.float32
    )


def positions_of(segment_row):
    earlier = jnp.sum((segment_row[None, :] < segment_row[:, None]).astype(jnp.int32), axis=1)
    return jnp.arange(segment_row.shape[0], dtype=jnp.int32) - earlier


def rope_tables(positions):
    half_dim = HD // 2
    inverse_freq = 10000.0 ** (-2.0 * jnp.arange(half_dim).astype(jnp.float32) / HD)
    angles = positions.astype(jnp.float32)[:, None] * inverse_freq[None, :]
    cos, sin = jnp.cos(angles), jnp.sin(angles)
    return jnp.concatenate([cos, cos], axis=1), jnp.concatenate([-sin, sin], axis=1)


def rotate(values, cos_table, sin_table):
    return values * cos_table + pltpu.roll(values, HD // 2, 1) * sin_table


def masked_scores(query_rot, key_rot, info):
    scores = contract_cols(query_rot, key_rot) * (1.0 / math.sqrt(HD))
    seg_col, row_col, seg_row, row_row = info
    allowed = (seg_col == seg_row) & (row_row <= row_col)
    return jnp.where(allowed, scores, -1e30)


def attend_kernel(
    rows_ref,
    query_weight,
    key_weight,
    value_weight,
    query_norm,
    key_norm,
    cos_ref,
    sin_ref,
    seg_col,
    row_col,
    seg_row,
    row_row,
    query_ref,
    key_ref,
    query_rot_ref,
    key_rot_ref,
    value_ref,
    attended_ref,
    total_ref,
):
    rows = rows_ref[...]
    cos_table, sin_table = cos_ref[...], sin_ref[...]
    info = (seg_col[...], row_col[...], seg_row[...], row_row[...])
    query_ref[...] = jnp.dot(rows, query_weight[...], preferred_element_type=jnp.float32)
    key_ref[...] = jnp.dot(rows, key_weight[...], preferred_element_type=jnp.float32)
    value_ref[...] = jnp.dot(
        rows, value_weight[...], preferred_element_type=jnp.float32
    ).astype(jnp.bfloat16)
    for head in range(query_ref.shape[1] // HD):
        span = slice(head * HD, (head + 1) * HD)
        queries, keys = query_ref[:, span], key_ref[:, span]
        query_rot = rotate(
            queries * inverse_rms(queries) * query_norm[:, span], cos_table, sin_table
        ).astype(jnp.bfloat16)
        key_rot = rotate(
            keys * inverse_rms(keys) * key_norm[:, span], cos_table, sin_table
        ).astype(jnp.bfloat16)
        query_rot_ref[:, span] = query_rot
        key_rot_ref[:, span] = key_rot
        scores = masked_scores(query_rot, key_rot, info)
        peak = jnp.max(scores, axis=-1, keepdims=True)
        shifted = jnp.exp(scores - peak)
        denominator = jnp.sum(shifted, axis=-1, keepdims=True)
        weights = (shifted / denominator).astype(jnp.bfloat16)
        attended_ref[:, span] = jnp.dot(
            weights, value_ref[:, span], preferred_element_type=jnp.float32
        ).astype(jnp.bfloat16)
        total_ref[head] = peak + jnp.log(denominator)


def attend_back_kernel(
    which_ref,
    row_grad_ref,
    output_weight,
    query_ref,
    key_ref,
    query_rot_ref,
    key_rot_ref,
    value_ref,
    total_ref,
    query_norm,
    key_norm,
    cos_ref,
    sin_ref,
    seg_col,
    row_col,
    seg_row,
    row_row,
    grad_query_ref,
    grad_key_ref,
    grad_value_ref,
    query_norm_grad,
    key_norm_grad,
):
    cos_table, sin_table = cos_ref[...], -sin_ref[...]
    info = (seg_col[...], row_col[...], seg_row[...], row_row[...])
    inv_sqrt = 1.0 / math.sqrt(HD)
    grad_attended = contract_cols(row_grad_ref[...], output_weight[...]).astype(jnp.bfloat16)

    def finish(grad_rot, raw, gain, out_ref, gain_ref, span):
        grad_norm = rotate(grad_rot, cos_table, sin_table)
        scale = inverse_rms(raw)
        hat = raw * scale
        gain_ref[:, span] = jnp.sum(grad_norm * hat, axis=0, keepdims=True)
        out_ref[:, span] = norm_backward(grad_norm * gain, hat, scale).astype(jnp.bfloat16)

    for head in range(query_ref.shape[1] // HD):
        span = slice(head * HD, (head + 1) * HD)
        query_rot, key_rot = query_rot_ref[:, span], key_rot_ref[:, span]
        grad_head = grad_attended[:, span]
        probs = jnp.exp(masked_scores(query_rot, key_rot, info) - total_ref[head])
        grad_weights = contract_cols(grad_head, value_ref[:, span])
        inner = jnp.sum(grad_weights * probs, axis=-1, keepdims=True)
        grad_scores = (probs * (grad_weights - inner)).astype(jnp.bfloat16)
        grad_value_ref[:, span] = contract_rows(probs.astype(jnp.bfloat16), grad_head).astype(
            jnp.bfloat16
        )
        grad_query_rot = (
            jnp.dot(grad_scores, key_rot, preferred_element_type=jnp.float32) * inv_sqrt
        )
        grad_key_rot = contract_rows(grad_scores, query_rot) * inv_sqrt
        finish(
            grad_query_rot,
            query_ref[:, span],
            query_norm[:, span],
            grad_query_ref,
            query_norm_grad,
            span,
        )
        finish(
            grad_key_rot, key_ref[:, span], key_norm[:, span], grad_key_ref, key_norm_grad, span
        )


def head_specs(length, width, model_width, wide):
    whole = pl.BlockSpec((length, model_width), lambda i: (0, 0))
    across = pl.BlockSpec((model_width, wide), lambda i: (0, i))
    down = pl.BlockSpec((wide, model_width), lambda i: (i, 0))
    heads = pl.BlockSpec((length, wide), lambda i: (0, i))
    gain = pl.BlockSpec((1, wide), lambda i: (0, i))
    total = pl.BlockSpec((wide // HD, length, 1), lambda i: (i, 0, 0))
    table = pl.BlockSpec((length, HD), lambda i: (0, 0))
    col = pl.BlockSpec((length, 1), lambda i: (0, 0))
    row = pl.BlockSpec((1, length), lambda i: (0, 0))
    return whole, across, down, heads, gain, total, [table, table, col, col, row, row]


def attend(rows, weights, gains, tables):
    length, model_width = rows.shape
    width = weights[0].shape[1]
    wide = min(2 * HD, width)
    whole, across, _, heads, gain, total, table_specs = head_specs(
        length, width, model_width, wide
    )
    low = jnp.bfloat16
    types = [jnp.float32, jnp.float32, low, low, low, low]
    return pl.pallas_call(
        attend_kernel,
        grid=(width // wide,),
        in_specs=[whole, across, across, across, gain, gain] + table_specs,
        out_specs=[heads] * 6 + [total],
        out_shape=[jax.ShapeDtypeStruct((length, width), t) for t in types]
        + [jax.ShapeDtypeStruct((width // HD, length, 1), jnp.float32)],
        cost_estimate=pl.CostEstimate(
            flops=18 * length * width * (model_width + length),
            bytes_accessed=2 * model_width * (length + 3 * width),
            transcendentals=width // HD * length * length,
        ),
        name="attend",
    )(rows, *weights, *gains, *tables)


def attend_back(which, row_grad, output_weight, saved, gains, tables, wide):
    length, model_width = row_grad.shape
    low = jnp.bfloat16
    whole = pl.BlockSpec((length, model_width), lambda i, w: (0, 0))
    down = pl.BlockSpec((wide, model_width), lambda i, w: (w[0], 0))
    heads = pl.BlockSpec((length, wide), lambda i, w: (0, w[0]))
    gain = pl.BlockSpec((1, wide), lambda i, w: (0, w[0]))
    total = pl.BlockSpec((wide // HD, length, 1), lambda i, w: (w[0], 0, 0))
    table = pl.BlockSpec((length, HD), lambda i, w: (0, 0))
    col = pl.BlockSpec((length, 1), lambda i, w: (0, 0))
    row = pl.BlockSpec((1, length), lambda i, w: (0, 0))
    out = pl.BlockSpec((length, wide), lambda i, w: (0, 0))
    gain_out = pl.BlockSpec((1, wide), lambda i, w: (0, 0))
    return pl.pallas_call(
        attend_back_kernel,
        grid_spec=pltpu.PrefetchScalarGridSpec(
            num_scalar_prefetch=1,
            grid=(1,),
            in_specs=[whole, down]
            + [heads] * 5
            + [total, gain, gain, table, table, col, col, row, row],
            out_specs=[out] * 3 + [gain_out] * 2,
        ),
        out_shape=[jax.ShapeDtypeStruct((length, wide), low)] * 3
        + [jax.ShapeDtypeStruct((1, wide), jnp.float32)] * 2,
        cost_estimate=pl.CostEstimate(
            flops=8 * length * wide * (model_width + 5 * length),
            bytes_accessed=2 * model_width * (length + wide) + 16 * length * wide,
            transcendentals=wide // HD * length * length,
        ),
        name="attend_back",
    )(which, row_grad, output_weight, *saved, *gains, *tables)


AXES = ("exp", "tp")


def after(value, others):
    return lax.optimization_barrier((value, others))[0]


class Links:
    def __init__(self, n_exp, n_tp):
        self.n_exp, self.n_tp, self.n_z = n_exp, n_tp, n_exp // 2

    def send(self, value, place):
        pairs = []
        for z in range(self.n_z):
            for x in range(2):
                for y in range(2):
                    for c in range(2):
                        z2, x2, y2, c2 = place(z, x, y, c)
                        pairs.append(((z * 2 + x) * 4 + y * 2 + c, (z2 * 2 + x2) * 4 + y2 * 2 + c2))
        return lax.ppermute(value, AXES, pairs)

    def core(self, value):
        return self.send(value, lambda z, x, y, c: (z, x, y, 1 - c))

    def flip_x(self, value):
        return self.send(value, lambda z, x, y, c: (z, 1 - x, y, c))

    def flip_y(self, value):
        return self.send(value, lambda z, x, y, c: (z, x, 1 - y, c))

    def first(self, value):
        return self.send(value, lambda z, x, y, c: (z, x ^ (1 - c), y ^ c, c))

    def second(self, value):
        return self.send(value, lambda z, x, y, c: (z, x ^ c, y ^ (1 - c), c))

    def along_z(self, value, steps):
        return self.send(value, lambda z, x, y, c: ((z + steps) % self.n_z, x, y, c))

    def flip_z(self, value, bit):
        return self.send(value, lambda z, x, y, c: (z ^ bit, x, y, c))

    def plane_groups(self):
        return [
            [(z * 2 + x) * 4 + t for x in range(2) for t in range(4)] for z in range(self.n_z)
        ]

    def spread(self, block, axis=0):
        near = jnp.concatenate([block, self.first(block)], axis=axis)
        plane = jnp.concatenate([near, self.second(near)], axis=axis)
        return plane, self.core(plane)

    def collect(self, plane, partner, kind):
        total = plane.astype(jnp.float32) + self.core(partner.astype(kind)).astype(jnp.float32)
        half = total.shape[0] // 2
        total = total[:half] + self.second(total[half:].astype(kind)).astype(jnp.float32)
        half = half // 2
        return total[:half] + self.first(total[half:].astype(kind)).astype(jnp.float32)

    def tp_rows(self, block):
        far = self.flip_y(block)
        return jnp.concatenate([block, self.core(block), far, self.core(far)], axis=0)

    def tp_sum(self, part):
        rows = part.shape[0] // 4
        sent = jnp.concatenate([part[rows : 2 * rows], part[3 * rows :]], axis=0)
        got = self.core(sent.astype(jnp.bfloat16)).astype(jnp.float32)
        far = part[2 * rows : 3 * rows] + got[rows:]
        return part[:rows] + got[:rows] + self.flip_y(far.astype(jnp.bfloat16)).astype(jnp.float32)

    def sum_exp(self, value):
        value = value + self.flip_x(value)
        for bit in range(self.n_z.bit_length() - 1):
            value = value + self.flip_z(value, 1 << bit)
        return value

    def sum_tp(self, value):
        value = value + self.core(value)
        return value + self.flip_y(value)


def gather_expert_rows(local_rows):
    return lax.all_gather(local_rows, "tp", axis=1, tiled=True)


def moe_slots(
    mixture_in, probabilities, grad_out, routes, capacity, gate_weight, up_weight, down_weight
):
    tok_rows, model_width = mixture_in.shape
    top_count = routes.shape[1]
    experts_all = probabilities.shape[1]
    expert_ids = jnp.arange(experts_all, dtype=jnp.int32)
    chosen = (routes[:, :, None] == expert_ids[None, None, :]).astype(jnp.float32)
    gate_values = jnp.sum(chosen * probabilities[:, None, :], axis=-1)
    assigned = routes.reshape(-1)
    matches = (assigned[:, None] == expert_ids[None, :]).astype(jnp.int32)
    earlier = jnp.sum(jnp.cumsum(matches, axis=0) * matches, axis=1) - 1
    slot_ids = jnp.where(earlier < capacity, assigned * capacity + earlier, experts_all * capacity)
    assign_count = tok_rows * top_count
    owners = (
        jnp.full((experts_all * capacity + 1,), assign_count, jnp.int32)
        .at[slot_ids]
        .set(jnp.arange(assign_count, dtype=jnp.int32))[:-1]
    )
    source_rows = owners // top_count
    input_pad = jnp.concatenate([mixture_in, jnp.zeros((1, model_width), jnp.bfloat16)], axis=0)
    outgoing = input_pad[source_rows].reshape(experts_all, capacity, model_width)
    arrived = lax.all_to_all(outgoing, "exp", split_axis=0, concat_axis=1, tiled=True)
    expert_in = gather_expert_rows(arrived)
    gate_pre = jnp.einsum(
        "erd,edf->erf", expert_in, gate_weight, preferred_element_type=jnp.float32
    )
    up_pre = jnp.einsum("erd,edf->erf", expert_in, up_weight, preferred_element_type=jnp.float32)
    hidden = (jax.nn.silu(gate_pre) * up_pre).astype(jnp.bfloat16)
    partial_out = jnp.einsum(
        "erf,efd->erd", hidden, down_weight, preferred_element_type=jnp.float32
    )
    returned = lax.psum_scatter(
        partial_out.astype(jnp.bfloat16), "tp", scatter_dimension=1, tiled=True
    )
    combined = lax.all_to_all(returned, "exp", split_axis=1, concat_axis=0, tiled=True)
    output_pad = jnp.concatenate(
        [combined.reshape(-1, model_width), jnp.zeros((1, model_width), jnp.bfloat16)], axis=0
    )
    expert_out = output_pad[slot_ids].astype(jnp.float32).reshape(tok_rows, top_count, model_width)
    mixture = jnp.sum(gate_values[:, :, None] * expert_out, axis=1)
    grad_gate = jnp.sum(grad_out[:, None, :] * expert_out, axis=-1)
    grad_sent = (
        (gate_values[:, :, None] * grad_out[:, None, :])
        .reshape(assign_count, model_width)
        .astype(jnp.bfloat16)
    )
    grad_pad = jnp.concatenate([grad_sent, jnp.zeros((1, model_width), jnp.bfloat16)], axis=0)
    grad_outgoing = grad_pad[owners].reshape(experts_all, capacity, model_width)
    grad_arrived = lax.all_to_all(grad_outgoing, "exp", split_axis=0, concat_axis=1, tiled=True)
    grad_expert = lax.all_gather(grad_arrived, "tp", axis=1, tiled=True)
    gate_pre = jnp.einsum(
        "erd,edf->erf", expert_in, gate_weight, preferred_element_type=jnp.float32
    )
    up_pre = jnp.einsum("erd,edf->erf", expert_in, up_weight, preferred_element_type=jnp.float32)
    gate_sig = jax.nn.sigmoid(gate_pre)
    gate_act = gate_pre * gate_sig
    hidden = (gate_act * up_pre).astype(jnp.bfloat16)
    grad_hidden = jnp.einsum(
        "erd,efd->erf", grad_expert, down_weight, preferred_element_type=jnp.float32
    )
    down_grad = jnp.einsum("erf,erd->efd", hidden, grad_expert, preferred_element_type=jnp.float32)
    grad_gate_pre = (grad_hidden * up_pre * gate_sig * (1.0 + gate_pre * (1.0 - gate_sig))).astype(
        jnp.bfloat16
    )
    grad_up_pre = (grad_hidden * gate_act).astype(jnp.bfloat16)
    gate_grad = jnp.einsum(
        "erd,erf->edf", expert_in, grad_gate_pre, preferred_element_type=jnp.float32
    )
    up_grad = jnp.einsum("erd,erf->edf", expert_in, grad_up_pre, preferred_element_type=jnp.float32)
    grad_in_part = jnp.einsum(
        "erf,edf->erd", grad_gate_pre, gate_weight, preferred_element_type=jnp.float32
    ) + jnp.einsum("erf,edf->erd", grad_up_pre, up_weight, preferred_element_type=jnp.float32)
    grad_in = lax.psum_scatter(
        grad_in_part.astype(jnp.bfloat16), "tp", scatter_dimension=1, tiled=True
    )
    grad_home = lax.all_to_all(grad_in, "exp", split_axis=1, concat_axis=0, tiled=True)
    home_pad = jnp.concatenate(
        [grad_home.reshape(-1, model_width), jnp.zeros((1, model_width), jnp.bfloat16)], axis=0
    )
    grad_assigned = home_pad[slot_ids].astype(jnp.float32).reshape(tok_rows, top_count, model_width)
    weighted = probabilities * jnp.sum(chosen * grad_gate[:, :, None], axis=1)
    return mixture, jnp.sum(grad_assigned, axis=1), weighted, gate_grad, up_grad, down_grad


def kept_experts(routes, experts_all, capacity):
    tok_rows = routes.shape[0]
    expert_ids = jnp.arange(experts_all, dtype=jnp.int32)
    member = jnp.sum((routes[:, :, None] == expert_ids[None, None, :]).astype(jnp.float32), axis=1)
    row = jnp.arange(tok_rows, dtype=jnp.int32)
    before = (row[None, :] < row[:, None]).astype(jnp.bfloat16)
    rank = jnp.dot(before, member.astype(jnp.bfloat16), preferred_element_type=jnp.float32)
    return jnp.where(rank < capacity, member, 0.0)


def expert_kernel(
    carried,
    place,
    ids_ref,
    *refs,
):
    blocks, refs = refs[:8], refs[8:]
    grads_hbm, kept_ref, router_ref, gate_hbm, up_hbm, down_hbm = refs[:6]
    (
        own_part,
        other_part,
        sum_ref,
        mix_all,
        rows_all,
        grad_all,
        hidden_all,
        gate_all,
        up_all,
        rows,
        grads,
        weights,
        down_w,
        mix,
        part,
        hidden_v,
        back_v,
        sem_in,
        sem_out,
    ) = refs[6 + carried :]
    local_experts, _, width = gate_hbm.shape
    block = blocks[0].shape[0]
    tile = 2 * block
    loads, stores = [], []

    def load(source, target):
        copy = pltpu.make_async_copy(source, target, sem_in.at[len(loads)])
        copy.start()
        loads.append(copy)
        return copy

    def store(source, target):
        copy = pltpu.make_async_copy(source, target, sem_out.at[len(stores)])
        copy.start()
        stores.append(copy)

    def load_rows(t):
        return [
            load(blocks[2 * t + i], rows.at[pl.ds(t * tile + i * block, block), :])
            for i in range(2)
        ]

    def load_grads(t):
        copies = []
        for i in range(2):
            at = pl.multiple_of(ids_ref[0, place // block + 2 * t + i] * block, block)
            copies.append(
                load(
                    grads_hbm.at[pl.ds(at, block), :],
                    grads.at[pl.ds(t * tile + i * block, block), :],
                )
            )
        return copies

    row_loads = [load_rows(0)]
    weight_loads = []
    for e in range(local_experts):
        weight_loads.append(
            [
                load(gate_hbm.at[e], weights.at[:, pl.ds(2 * e * width, width)]),
                load(up_hbm.at[e], weights.at[:, pl.ds((2 * e + 1) * width, width)]),
            ]
        )
        if e == 0:
            grad_loads = [load_grads(0)]
            down_load = load(down_hbm, down_w)
    for t in range(1, 4):
        row_loads.append(load_rows(t))
        grad_loads.append(load_grads(t))

    for t in range(4):
        at = pl.ds(t * tile, tile)
        span = slice(t * tile, (t + 1) * tile)
        whole = pl.ds(place + t * tile, tile)
        half = pl.ds((t % 2) * tile, tile)
        for copy in row_loads[t]:
            copy.wait()
        store(rows.at[at, :], rows_all.at[whole, :])
        x = rows[span, :]
        logits = jnp.dot(x, router_ref[...], preferred_element_type=jnp.float32)
        shifted = jnp.exp(logits - jnp.max(logits, axis=-1, keepdims=True))
        gates = shifted[:, :local_experts] / jnp.sum(shifted, axis=-1, keepdims=True)
        gates = gates * kept_ref[span, :]
        sums = []
        for e in range(local_experts):
            low, mid, high = 2 * e * width, (2 * e + 1) * width, (2 * e + 2) * width
            here = slice(e * width, (e + 1) * width)
            gate = gates[:, e : e + 1]
            if t == 0:
                for copy in weight_loads[e]:
                    copy.wait()
            pre = jnp.dot(x, weights[:, low:high], preferred_element_type=jnp.float32)
            gate_pre, up_pre = pre[:, :width], pre[:, width:]
            if e == 0:
                for copy in grad_loads[t]:
                    copy.wait()
                store(grads.at[at, :], grad_all.at[whole, :])
                if t == 0:
                    down_load.wait()
            back = contract_cols(grads[span, :], down_w[here, :]) * gate
            sig = jax.nn.sigmoid(gate_pre)
            act = gate_pre * sig
            hidden = (act * up_pre).astype(jnp.bfloat16).astype(jnp.float32)
            sums.append(jnp.sum(hidden * back, axis=-1, keepdims=True))
            hidden_v[span, here] = (hidden * gate).astype(jnp.bfloat16)
            back_v[span, low:mid] = (
                back * up_pre * sig * (1.0 + gate_pre * (1.0 - sig))
            ).astype(jnp.bfloat16)
            back_v[span, mid:high] = (back * act).astype(jnp.bfloat16)
            store(back_v.at[at, pl.ds(low, width)], gate_all.at[e, whole, :])
            store(back_v.at[at, pl.ds(mid, width)], up_all.at[e, whole, :])
        store(hidden_v.at[at, :], hidden_all.at[whole, :])
        sum_ref[span, :] = jnp.concatenate(sums, axis=1)
        part[span, :] = contract_cols(back_v[span, :], weights[...]).astype(jnp.bfloat16)
        store(part.at[at, :], (own_part if t < 2 else other_part).at[half, :])
        mix[span, :] = jnp.dot(
            hidden_v[span, :], down_w[...], preferred_element_type=jnp.float32
        ).astype(jnp.bfloat16)
        for i in range(2):
            home = pl.multiple_of(ids_ref[1, place // block + 2 * t + i] * block, block)
            store(
                mix.at[pl.ds(t * tile + i * block, block), :], mix_all.at[pl.ds(home, block), :]
            )
    for copy in stores:
        copy.wait()


def run_experts(
    place, count, ids, blocks, grads, kept, router, gate_weight, up_weight, down_flat, carried
):
    block, model_width = blocks[0].shape
    local_experts, _, width = gate_weight.shape
    flat = local_experts * width
    tok_count = 8 * block
    whole = tok_count * count
    low = jnp.bfloat16
    hbm = pl.BlockSpec(memory_space=pl.ANY)
    vmem = pl.BlockSpec(memory_space=pltpu.VMEM)
    plane = jax.ShapeDtypeStruct((tok_count // 2, model_width), low)
    out = pl.pallas_call(
        functools.partial(expert_kernel, len(carried), place * tok_count),
        in_specs=[pl.BlockSpec(memory_space=pltpu.SMEM)]
        + [hbm] * 9
        + [vmem] * 2
        + [hbm] * (3 + len(carried)),
        out_specs=[hbm] * 2 + [vmem] + [hbm] * 6,
        out_shape=[plane] * 2
        + [
            jax.ShapeDtypeStruct((tok_count, local_experts), jnp.float32),
            jax.ShapeDtypeStruct((whole, model_width), low),
            jax.ShapeDtypeStruct((whole, model_width), low),
            jax.ShapeDtypeStruct((whole, model_width), low),
            jax.ShapeDtypeStruct((whole, flat), low),
            jax.ShapeDtypeStruct((local_experts, whole, width), low),
            jax.ShapeDtypeStruct((local_experts, whole, width), low),
        ],
        scratch_shapes=[
            pltpu.VMEM((tok_count, model_width), low),
            pltpu.VMEM((tok_count, model_width), low),
            pltpu.VMEM((model_width, 2 * flat), low),
            pltpu.VMEM(down_flat.shape, low),
            pltpu.VMEM((tok_count, model_width), low),
            pltpu.VMEM((tok_count, model_width), low),
            pltpu.VMEM((tok_count, flat), low),
            pltpu.VMEM((tok_count, 2 * flat), low),
            pltpu.SemaphoreType.DMA((17 + 2 * local_experts,)),
            pltpu.SemaphoreType.DMA((4 * (6 + 2 * local_experts),)),
        ],
        input_output_aliases={15 + i: 3 + i for i in range(len(carried))},
        cost_estimate=pl.CostEstimate(
            flops=25 * tok_count * model_width * flat,
            bytes_accessed=12 * model_width * (tok_count + flat),
            transcendentals=tok_count * flat,
        ),
        name="experts",
    )(ids, *blocks, grads, kept, router, gate_weight, up_weight, down_flat, *carried)
    return out[:3], list(out[3:])


class HalfSum:
    def __init__(self, links, value):
        self.links, self.value = links, value
        self.bits = [1 << b for b in range(links.n_z.bit_length() - 1)]

    def stages(self):
        return 2 * len(self.bits)

    def go(self, stage, ties=()):
        links, value, count = self.links, self.value, len(self.bits)
        z = lax.axis_index("exp") // 2
        if stage < count:
            bit = self.bits[stage]
            upper = (z // bit) % 2
            half = value.shape[0] // 2
            kept = lax.dynamic_slice_in_dim(value, upper * half, half, axis=0)
            sent = lax.dynamic_slice_in_dim(value, (1 - upper) * half, half, axis=0)
            got = links.flip_z(after(sent.astype(jnp.bfloat16), ties), bit)
            value = kept + got.astype(jnp.float32)
            if stage == count - 1:
                value = value.astype(jnp.bfloat16)
        else:
            bit = self.bits[2 * count - 1 - stage]
            got = links.flip_z(after(value, ties), bit)
            value = jnp.where(
                (z // bit) % 2 == 0,
                jnp.concatenate([value, got], axis=0),
                jnp.concatenate([got, value], axis=0),
            )
        self.value = value
        return got


class Spread:
    def __init__(self, links, block, order):
        self.links, self.order, self.own = links, order, block
        self.blocks, self.near, self.far, self.other = {}, {}, {}, {}

    def go_z(self, k, ties=()):
        block = self.own
        if self.order[k]:
            block = self.links.along_z(after(block, ties), self.order[k])
        self.blocks[k] = block
        return block

    def go_near(self, k, ties=()):
        block = after(self.blocks[k], ties)
        self.near[k] = [self.links.first(block), self.links.second(block)]
        return self.near[k]

    def go_far(self, k, ties=()):
        self.far[k] = self.links.second(after(self.near[k][0], ties))
        return self.far[k]

    def go_core(self, k, ties=()):
        plane = after(self.plane(k), ties)
        self.other[k] = [self.links.core(block) for block in plane]
        return self.other[k]

    def plane(self, k):
        return [self.blocks[k], *self.near[k], self.far[k]]

    def eight(self, k):
        return self.plane(k) + self.other[k]


def source_ids(links, order):
    n_z = links.n_z
    table, homes = [], []
    for z, x, y, c in itertools.product(range(n_z), range(2), range(2), range(2)):
        row, home = [], []
        for k, r in enumerate(order):
            for core in (c, 1 - c):
                for dx, dy in [(0, 0), (1 - core, core), (core, 1 - core), (1, 1)]:
                    member = (x ^ dx) * 4 + (y ^ dy) * 2 + core
                    row.append(member if k == 0 else member * (n_z - 1) + k - 1)
                    home.append((z - r) % n_z * 8 + member)
        table.append(row)
        homes.append(home)
    here = lax.axis_index(AXES)
    return jnp.asarray([table, homes], jnp.int32)[:, here]


class Gathering:
    def __init__(self, links, order):
        self.links, self.order, self.terms = links, order, {}

    def total(self, k, first, last):
        wide = [t[first:last].astype(jnp.float32) for t in self.terms[k]]
        return functools.reduce(jnp.add, wide)

    def go_core(self, k, own, partner, ties=()):
        self.terms[k] = [own, self.links.core(after(partner, ties))]
        return self.terms[k][-1]

    def go_second(self, k, ties=()):
        rows = self.terms[k][0].shape[0]
        sent = self.total(k, rows // 2, rows).astype(jnp.bfloat16)
        self.terms[k].append(self.links.second(after(sent, ties)))
        return self.terms[k][-1]

    def go_first(self, k, ties=()):
        rows = self.terms[k][0].shape[0]
        sent = self.total(k, rows // 4, rows // 2).astype(jnp.bfloat16)
        self.terms[k].append(self.links.first(after(sent, ties)))
        return self.terms[k][-1]

    def go_z(self, k, ties=()):
        rows = self.terms[k][0].shape[0]
        sent = self.total(k, 0, rows // 4)
        if self.order[k]:
            sent = self.links.along_z(after(sent.astype(jnp.bfloat16), ties), -self.order[k])
        self.terms[k] = [sent]
        return sent

    def home(self):
        return functools.reduce(
            jnp.add, [self.terms[k][0].astype(jnp.float32) for k in range(len(self.order))]
        )


def moe_dense(
    links,
    order,
    attention_in,
    mixture_in,
    grads,
    kept_chunks,
    router_weight,
    gate_weight,
    up_weight,
    down_weight,
):
    tok_rows, model_width = mixture_in.shape
    local_experts, _, hidden_width = gate_weight.shape
    experts_all = router_weight.shape[1]
    first_expert = lax.axis_index("exp") * local_experts
    down_flat = down_weight.reshape(local_experts * hidden_width, model_width)
    router = jnp.roll(router_weight, -first_expert, axis=1)
    n_z = links.n_z
    ids = source_ids(links, order)
    kept_own = [
        lax.dynamic_slice_in_dim(
            jnp.concatenate(kept_chunks[r]), first_expert, local_experts, axis=1
        )
        for r in order
    ]
    rows = Spread(links, mixture_in, order)
    back = Gathering(links, order)
    carried = []
    done = [None] * n_z

    def experts(k, ties):
        nonlocal carried
        done[k], carried = run_experts(
            k,
            n_z,
            ids,
            rows.eight(k),
            grads[k],
            after(kept_own[k], ties),
            router,
            gate_weight,
            up_weight,
            down_flat,
            carried,
        )

    rows.go_z(0)
    held = [rows.go_z(1)]
    held.append(rows.go_z(2, held))
    held.append(rows.go_z(3, held))
    rows.go_near(0)
    rows.go_far(0)
    rows.go_core(0)
    held += rows.go_near(1, [rows.blocks[1]])
    pin = rows.near[1]
    for k in range(n_z):
        experts(k, held)
        held = []
        if k + 1 < n_z:
            rows.go_far(k + 1, pin)
        if k + 2 < n_z:
            held += rows.go_near(k + 2, pin)
        pin = [done[k][2]]
        if k + 1 < n_z:
            rows.go_core(k + 1, pin)
        if k == 0:
            held.append(back.go_core(0, done[0][0], done[0][1]))
        elif k == 1:
            held.append(back.go_second(0, [done[0][2]]))
        elif k == 2:
            held.append(back.go_core(1, done[1][0], done[1][1], [done[1][2]]))
            held.append(back.go_first(0, [done[1][2]]))
    mix_all = carried[0]
    step_zero = [
        back.go_second(1, [done[2][2]]),
        back.go_core(2, done[2][0], done[2][1], [done[2][2]]),
        back.go_z(0, [done[2][2]]),
    ]
    step_one = [
        back.go_core(3, done[3][0], done[3][1]),
        back.go_second(2, step_zero),
        back.go_first(1, step_zero),
    ]
    step_two = [
        back.go_second(3, step_one),
        back.go_first(2, step_one),
        back.go_z(1, step_one),
    ]
    early_x = links.flip_x(after(attention_in, step_two))
    step_three = [back.go_first(3), back.go_z(2, step_two), early_x]
    far_x = links.flip_y(after(early_x, step_three))
    back.go_z(3)
    input_grad = after(back.home(), far_x)
    peer_rows = jnp.concatenate(
        [early_x, links.core(early_x), far_x, links.core(far_x)], axis=0
    )
    full = []
    for half in range(2):
        planes = []
        for k in range(n_z):
            local = done[k][2].reshape(2, -1, tok_rows, local_experts)[half].transpose(0, 2, 1)
            zero = jnp.zeros((local.shape[0], experts_all, tok_rows), jnp.float32)
            planes.append(lax.dynamic_update_slice_in_dim(zero, local, first_expert, axis=1))
        full.append(jnp.stack(planes, axis=1))
    small = links.collect(full[0], full[1], jnp.float32)[0]
    weighted = functools.reduce(
        jnp.add,
        [links.along_z(small[k], -r) if r else small[k] for k, r in enumerate(order)],
    )
    return mix_all, peer_rows, input_grad, weighted.T, carried[1:]


def expert_weight_grad(saved, which, ties):
    rows_all, grad_all, hidden_all, gate_all, up_all = saved
    if which == 2:
        down_grad = contract_rows(after(hidden_all, ties), grad_all)
        return down_grad.reshape(gate_all.shape[0], gate_all.shape[2], grad_all.shape[1])
    parts = after((gate_all, up_all)[which], ties)
    return jnp.stack([contract_rows(rows_all, parts[e]) for e in range(parts.shape[0])])


def body(
    mesh_sizes,
    tokens,
    cotangent,
    attention_gain,
    query_weight,
    key_weight,
    value_weight,
    output_weight,
    query_norm,
    key_norm,
    mixture_gain,
    router_weight,
    gate_weight,
    up_weight,
    down_weight,
    routes,
    segments,
):
    tok_rows, model_width = tokens.shape
    top_count = routes.shape[1]
    experts_all = router_weight.shape[1]
    capacity = tok_rows * top_count * 7 // (8 * experts_all)
    local_width = query_weight.shape[1]
    n_exp, n_tp = mesh_sizes
    dense = experts_all <= 2 * top_count and n_tp == 4 and n_exp == 8
    links = Links(n_exp, n_tp)
    grad_out = cotangent.astype(jnp.float32)
    if dense:
        kept = kept_experts(routes, experts_all, capacity).T.astype(jnp.bfloat16)
        kept_z = jnp.stack([kept] + [links.along_z(kept, r) for r in range(1, n_exp // 2)])
        kept_planes = links.spread(kept_z[None])
        kept_chunks = [
            [
                plane[:, r].transpose(0, 2, 1).reshape(-1, experts_all).astype(jnp.float32)
                for plane in kept_planes
            ]
            for r in range(n_exp // 2)
        ]
        order = [0, 2, 1, 3]
        groups = links.plane_groups()
        near_grads = lax.all_gather(
            cotangent, AXES, axis=0, tiled=True, axis_index_groups=groups
        )
        moved = [links.along_z(cotangent, r) for r in order[1:]]
    inputs = tokens.astype(jnp.float32)
    scale_one = inverse_rms(inputs)
    normed_one = inputs * scale_one
    attention_in = (normed_one * attention_gain).astype(jnp.bfloat16)
    segment_row = segments[0]
    tp_order = lax.axis_index("tp") ^ jnp.arange(n_tp, dtype=jnp.int32)
    positions = positions_of(segment_row).reshape(n_tp, tok_rows)[tp_order].reshape(-1)
    segment_rel = segment_row.reshape(n_tp, tok_rows)[tp_order].reshape(-1)
    row_rel = (
        tp_order[:, None] * tok_rows + jnp.arange(tok_rows, dtype=jnp.int32)[None, :]
    ).reshape(-1)
    tables = (
        *rope_tables(positions),
        segment_rel[:, None],
        row_rel[:, None],
        segment_rel[None, :],
        row_rel[None, :],
    )
    gains = (query_norm[None, :], key_norm[None, :])
    gathered_rows = links.tp_rows(attention_in)
    *saved, attended, log_totals = attend(
        gathered_rows, (query_weight, key_weight, value_weight), gains, tables
    )
    if dense:
        far_grads = jnp.concatenate(after(moved, [attended, near_grads]), axis=0)
        far_grads = lax.all_gather(
            far_grads, AXES, axis=0, tiled=True, axis_index_groups=groups
        )
        grads = [near_grads] + [far_grads] * 3
    attention_block = links.tp_sum(
        jnp.dot(attended, output_weight, preferred_element_type=jnp.float32)
    )
    middle = inputs + attention_block
    scale_two = inverse_rms(middle)
    normed_two = middle * scale_two
    mixture_in = (normed_two * mixture_gain).astype(jnp.bfloat16)
    logits = jnp.dot(mixture_in, router_weight, preferred_element_type=jnp.float32)
    probabilities = jax.nn.softmax(logits, axis=-1)
    if dense:
        mix_all, peer_rows, grad_expert_in, weighted, expert_saved = moe_dense(
            links,
            order,
            attention_in,
            mixture_in,
            grads,
            kept_chunks,
            router_weight,
            gate_weight,
            up_weight,
            down_weight,
        )
    else:
        mixture, grad_expert_in, weighted, gate_grad, up_grad, down_grad = moe_slots(
            mixture_in,
            probabilities,
            grad_out,
            routes,
            capacity,
            gate_weight,
            up_weight,
            down_weight,
        )
        peer_rows = links.tp_rows(links.flip_x(attention_in))
    grad_logits = weighted - probabilities * jnp.sum(weighted, axis=-1, keepdims=True)
    router_grad = jnp.dot(mixture_in.astype(jnp.float32).T, grad_logits, precision=HIGH)
    grad_mixture_in = grad_expert_in + jnp.dot(
        grad_logits, router_weight.astype(jnp.float32).T, precision=HIGH
    )
    mixture_gain_grad = jnp.sum(grad_mixture_in * normed_two, axis=0)
    grad_middle = grad_out + norm_backward(grad_mixture_in * mixture_gain, normed_two, scale_two)
    grad_attention = grad_middle.astype(jnp.bfloat16)
    row_grad = links.tp_rows(grad_attention)
    wide = local_width // 2
    side = lax.axis_index("exp") % 2
    own_cols = lax.dynamic_slice_in_dim(attended, side * wide, wide, axis=1)
    other_cols = lax.dynamic_slice_in_dim(attended, (1 - side) * wide, wide, axis=1)
    held = []
    results = [None, None]
    for turn in range(2):
        which = 1 - side if turn == 0 else side
        ties = [r[0] for r in results[:turn]]
        if turn == 1:
            ties += held
        results[turn] = attend_back(
            after(which.astype(jnp.int32)[None], ties),
            row_grad,
            output_weight,
            (*saved, log_totals),
            gains,
            tables,
            wide,
        )
    other = jnp.concatenate(results[0][:3], axis=1)
    peer_grads = links.flip_x(other)
    if dense:
        mixture = lax.psum_scatter(
            after(mix_all, peer_grads), AXES, scatter_dimension=0, tiled=True
        )
    other_half = contract_rows(other_cols, row_grad).astype(jnp.bfloat16)
    other_half = links.flip_x(after(other_half, peer_grads))
    own_grads = jnp.concatenate(results[1][:3], axis=1)

    def in_order(own_part, other_part, axis):
        return jnp.where(
            side == 0,
            jnp.concatenate([own_part, other_part], axis=axis),
            jnp.concatenate([other_part, own_part], axis=axis),
        )

    grad_queries, grad_keys, grad_values, query_norm_grad, key_norm_grad = [
        in_order(results[1][i], results[0][i], 1) for i in range(5)
    ]
    query_norm_grad, key_norm_grad = query_norm_grad[0], key_norm_grad[0]
    total_grad = contract_cols(grad_queries, query_weight)
    total_grad = total_grad + contract_cols(grad_keys, key_weight)
    total_grad = total_grad + contract_cols(grad_values, value_weight)
    grad_attention_in = links.tp_sum(total_grad)
    pieces = []
    for i in range(3):
        span = slice(i * wide, (i + 1) * wide)
        total = contract_rows(gathered_rows, own_grads[:, span])
        pieces.append(HalfSum(links, total + contract_rows(peer_rows, peer_grads[:, span])))
    pieces.append(
        HalfSum(links, contract_rows(own_cols, row_grad) + other_half.astype(jnp.float32))
    )
    ties = [pieces[0].go(0)]
    attention_gain_grad = jnp.sum(grad_attention_in * normed_one, axis=0)
    tokens_grad = grad_middle + norm_backward(
        grad_attention_in * attention_gain, normed_one, scale_one
    )
    if dense:
        sums = jnp.concatenate(
            [
                query_norm_grad,
                key_norm_grad,
                attention_gain_grad,
                mixture_gain_grad,
                router_grad.reshape(-1),
            ]
        )
    flips = [
        links.flip_x,
        lambda v: links.flip_z(v, 1),
        lambda v: links.flip_z(v, 2),
        links.core,
        links.flip_y,
    ]
    stages = pieces[0].stages()
    big_sums = [None] * 4
    expert_grads = []
    for step in range(stages + 3):
        moved = []
        for p in range(4):
            stage = step + 1 - p
            if 0 <= stage < stages:
                moved.append(pieces[p].go(stage, ties))
            elif stage == stages:
                whole = pieces[p].value
                got = links.flip_x(after(whole, ties))
                big_sums[p] = in_order(whole, got, 1 if p < 3 else 0).astype(jnp.float32)
                moved.append(big_sums[p])
        if dense and step < 5:
            got = flips[step](after(sums, ties))
            if step > 2:
                got = jnp.concatenate([jnp.zeros_like(got[: 2 * local_width]), got[2 * local_width :]])
            sums = sums + got
            moved.append(sums)
        if dense and step in (1, 3, 5):
            expert_grads.append(expert_weight_grad(expert_saved, step // 2, ties))
            moved.append(expert_grads[-1])
        ties = moved
    query_weight_grad, key_weight_grad, value_weight_grad, output_weight_grad = big_sums
    if dense:
        gate_grad, up_grad, down_grad = expert_grads
    output = (middle + mixture).astype(jnp.bfloat16)
    if dense:
        norm_sums = (sums[:local_width], sums[local_width : 2 * local_width])
        sums = sums[2 * local_width :]
        shared_sums = (
            sums[:model_width],
            sums[model_width : 2 * model_width],
            sums[2 * model_width :].reshape(model_width, experts_all),
        )
    else:
        norm_sums = [
            lax.psum(value.astype(jnp.bfloat16), "exp").astype(jnp.float32)
            for value in (query_norm_grad, key_norm_grad)
        ]
        shared_sums = lax.psum((attention_gain_grad, mixture_gain_grad, router_grad), AXES)
    return (
        output,
        tokens_grad,
        shared_sums[0],
        query_weight_grad,
        key_weight_grad,
        value_weight_grad,
        output_weight_grad,
        norm_sums[0],
        norm_sums[1],
        shared_sums[1],
        shared_sums[2],
        gate_grad,
        up_grad,
        down_grad,
    )


def solution(mesh):
    return jax.shard_map(
        functools.partial(body, (mesh.shape["exp"], mesh.shape["tp"])),
        mesh=mesh,
        in_specs=(
            P(("exp", "tp"), None),
            P(("exp", "tp"), None),
            P(),
            P(None, "tp"),
            P(None, "tp"),
            P(None, "tp"),
            P("tp", None),
            P("tp"),
            P("tp"),
            P(),
            P(),
            P("exp", None, "tp"),
            P("exp", None, "tp"),
            P("exp", "tp", None),
            P(("exp", "tp"), None),
            P("exp", None),
        ),
        out_specs=(
            P(("exp", "tp"), None),
            P(("exp", "tp"), None),
            P(),
            P(None, "tp"),
            P(None, "tp"),
            P(None, "tp"),
            P("tp", None),
            P("tp"),
            P("tp"),
            P(),
            P(),
            P("exp", None, "tp"),
            P("exp", None, "tp"),
            P("exp", "tp", None),
        ),
        check_vma=False,
    )
```
